512 devices in a mesh: row: 16 (over y, core), col: 32 (over z, x).
Axes of the slice: x: 4, y: 8, z: 8, core: 2. Of those that a mesh axis runs over, the one named last changes fastest.
Arguments:
- query_matrix: bfloat16 [128, 512, 768], P('row', 'col'), may hold values from -6 to 16.133757
- key_matrix: bfloat16 [128, 512, 768], P('row', 'col'), may hold values from -6 to 6
- value_matrix: bfloat16 [128, 512, 768], P('row', 'col'), may hold values from -6 to 6
- tissue: int32 [128, 512], replicated, may hold values 0 or 1
- dilation_levels: int32 [16], replicated, may hold values from 0 to 2
- segment_levels: int32 [16], replicated, may hold values from 0 to 2
- output_matrix: bfloat16 [768, 768], replicated, may hold values from -0.21875 to 0.21875
Outputs:
- encoded: bfloat16 [128, 512, 768], P('row', 'col')
The draws below stay inside these ranges and needn't reach their ends.
Inputs may be any that keep to these rules, and one draw needn't show every extreme that they name: 1 marks a tissue tile, 0 background. Head h uses the dilation 8 * 2^dilation_levels[h]. Head h uses segments of 512 / 2^segment_levels[h] tiles of a grid row.
All inputs are finite; a program needn't handle non-finite values.
Results may differ from the reference program's by a relative error of at most 0.0055.
Values may be sent and summed in bfloat16 or wider, within the bound.
No kernel may reach another device: no remote copies, remote signals or barrier semaphores. Data moves between devices by JAX's collectives and lax.ppermute only.
A program may use at most 64 MiB of HBM per device.

```python
import math
import jax
import jax.numpy as jnp
import numpy as np
from jax import lax

D = 768
HEAD_COUNT = 16
DEVICE_GRID_ROWS = 8
DEVICE_GRID_COLS = 16
R = 8
DILATION_MIN = 8
GRID_ROWS = 128
GRID_COLUMNS = 512
REACHED_TILES = 64
N_ROW = 16
N_COL = 32


def draw_query_matrix(key, part):
    noise_key = jax.random.fold_in(key, 0)
    drawn = jnp.clip(jax.random.normal(noise_key, (GRID_ROWS, GRID_COLUMNS, D), jnp.float32), -6.0, 6.0)
    return drawn.astype(jnp.bfloat16)


def draw_key_matrix(key, part):
    noise_key = jax.random.fold_in(key, 7)
    drawn = jnp.clip(jax.random.normal(noise_key, (GRID_ROWS, GRID_COLUMNS, D), jnp.float32), -6.0, 6.0)
    return drawn.astype(jnp.bfloat16)


def with_ends(values, own_key, low, top_value):
    longest = values.shape.index(max(values.shape))
    spots = []
    for shift in (0, 1):
        where = [jax.random.randint(jax.random.fold_in(own_key, axis), (), 0, length) for axis, length in enumerate(values.shape)]
        where[longest] = (where[longest] + shift) % values.shape[longest]
        spots.append(tuple(where))
    return values.at[spots[0]].set(low).at[spots[1]].set(top_value)


def levels(key, shape, cuts, low, high):
    def one(axis_at, shards_of):
        draws = jax.random.uniform(jax.random.fold_in(jax.random.fold_in(key, 6), axis_at), (shards_of,), jnp.float32, low / len(cuts), high / len(cuts))
        return jnp.repeat(jnp.exp(draws), shape[axis_at] // shards_of).reshape((-1,) + (1,) * (len(shape) - axis_at - 1))

    level = one(*cuts[0])
    for cut in cuts[1:]:
        level = level * one(*cut)
    return level


def normal_values(stream_key, shape, scale, reach, cuts=(), held_as=jnp.bfloat16):
    level = levels(stream_key, shape, cuts, -0.22, 0.18) if cuts else 1.0
    drawn = jax.random.normal(stream_key, shape, jnp.float32) * scale * level
    return jnp.minimum(jnp.maximum(drawn, -reach), reach).astype(held_as)


def setup_inputs(seed: int = 0) -> dict:
    keys = jax.random.split(jax.random.key(seed), 8)
    query_matrix = draw_query_matrix(jax.random.fold_in(keys[7], 71), 0)
    key_matrix = draw_key_matrix(jax.random.fold_in(keys[7], 71), 0)
    value_matrix = normal_values(keys[2], (GRID_ROWS, GRID_COLUMNS, D), 1.0, 6.0, ((0, 16), (1, 32)))
    tissue = with_ends((jax.random.randint(keys[3], (GRID_ROWS, GRID_COLUMNS), 0, 5) < 3).astype(jnp.int32), jax.random.fold_in(keys[3], 1), 0, 1)
    dilation_levels = with_ends(jax.random.randint(keys[4], (HEAD_COUNT,), 0, 3), jax.random.fold_in(keys[4], 1), 0, 2).astype(jnp.int32)
    segment_levels = with_ends(jax.random.randint(keys[5], (HEAD_COUNT,), 0, 3), jax.random.fold_in(keys[5], 1), 0, 2).astype(jnp.int32)
    output_matrix = normal_values(keys[6], (D, D), D ** -0.5, 0.21875)
    return dict(query_matrix=query_matrix, key_matrix=key_matrix, value_matrix=value_matrix, tissue=tissue, dilation_levels=dilation_levels, segment_levels=segment_levels, output_matrix=output_matrix)


NEG_FILL = -1e+30

def window_static(device_rows, device_columns):
    region_rows = np.arange(device_rows + 2 * R) - R
    query_rows = np.arange(device_rows)
    region_cols = np.arange(device_columns + 2 * R) - R
    query_cols = np.arange(device_columns)
    near_rows = np.abs(region_rows[None, :] - query_rows[:, None]) <= R
    near_cols = np.abs(region_cols[None, :] - query_cols[:, None]) <= R
    same_rows = region_rows[None, :] == query_rows[:, None]
    same_cols = region_cols[None, :] == query_cols[:, None]
    near_both = near_rows[:, None, :, None] & near_cols[None, :, None, :]
    self_both = same_rows[:, None, :, None] & same_cols[None, :, None, :]
    return (near_both, self_both)

def window_part(queries, key_region, value_region, permitted_mask, group_size):
    head_dimension = queries.shape[-1] // HEAD_COUNT
    scale = 1.0 / math.sqrt(head_dimension)
    numerators, maxima, totals = ([], [], [])
    for head_first in range(0, HEAD_COUNT, group_size):
        lower = head_first * head_dimension
        upper = (head_first + group_size) * head_dimension
        query_grp = queries[:, lower:upper].reshape(queries.shape[0], group_size, head_dimension).astype(jnp.float32)
        key_grp = key_region[:, lower:upper].reshape(key_region.shape[0], group_size, head_dimension).astype(jnp.float32)
        value_grp = value_region[:, lower:upper].reshape(value_region.shape[0], group_size, head_dimension).astype(jnp.float32)
        scores = jnp.einsum('qhd,khd->hqk', query_grp, key_grp) * scale
        scores = jnp.where(permitted_mask[None], scores, NEG_FILL)
        highest = lax.optimization_barrier(jnp.max(scores, axis=-1))
        exp_terms = jnp.exp(scores - highest[..., None])
        totals.append(lax.optimization_barrier(jnp.sum(exp_terms, axis=-1)))
        rounded = lax.optimization_barrier(exp_terms.astype(jnp.bfloat16))
        numerators.append(jnp.einsum('hqk,khd->qhd', rounded.astype(jnp.float32), value_grp))
        maxima.append(highest)
    return (jnp.concatenate(numerators, axis=1), jnp.concatenate(maxima, axis=0).T, jnp.concatenate(totals, axis=0).T)

def dilation_valid_mask(tissue, row_indices, head_indices, column_indices, dilation_levels, segment_levels, selected_count, column_total):
    key_columns = jnp.arange(selected_count, dtype=jnp.int32)[None, :] * DILATION_MIN + (head_indices % DILATION_MIN)[:, None]
    tissue_keys = tissue[row_indices[:, None], key_columns]
    dilation_stride = jnp.left_shift(jnp.int32(DILATION_MIN), dilation_levels[head_indices])
    segment = jnp.right_shift(jnp.int32(column_total), segment_levels[head_indices])
    phase_ok = key_columns % dilation_stride[:, None] == (head_indices % dilation_stride)[:, None]
    key_seg = key_columns // segment[:, None]
    query_seg = column_indices[None, :] // segment[:, None]
    same_seg = key_seg[:, None, :] == query_seg[:, :, None]
    return same_seg & ((tissue_keys == 1) & phase_ok)[:, None, :]

def dilation_partial(queries, keys_sel, values_sel, permitted_mask):
    scale = 1.0 / math.sqrt(queries.shape[-1])
    scores = jnp.einsum('icw,isw->ics', queries.astype(jnp.float32), keys_sel.astype(jnp.float32)) * scale
    scores = jnp.where(permitted_mask, scores, NEG_FILL)
    highest = lax.optimization_barrier(jnp.max(scores, axis=-1))
    exp_terms = jnp.where(permitted_mask, jnp.exp(scores - highest[..., None]), 0.0)
    totals = lax.optimization_barrier(jnp.sum(exp_terms, axis=-1))
    rounded = lax.optimization_barrier(exp_terms.astype(jnp.bfloat16))
    softmax_numer = jnp.einsum('ics,isw->icw', rounded.astype(jnp.float32), values_sel.astype(jnp.float32))
    return (softmax_numer, highest, totals)

def merge_partials(neighbour_numer, neighbour_max, neighbour_sum, dilation_numer, dilation_score_max, dilation_sum):
    running_maximum = jnp.maximum(neighbour_max, dilation_score_max)
    neighbour_rescale = jnp.exp(neighbour_max - running_maximum)
    dilation_rescale = jnp.exp(dilation_score_max - running_maximum)
    softmax_numer = neighbour_rescale[..., None] * neighbour_numer + dilation_rescale[..., None] * dilation_numer
    softmax_denom = neighbour_rescale * neighbour_sum + dilation_rescale * dilation_sum
    return softmax_numer / softmax_denom[..., None]

def reference(query_matrix, key_matrix, value_matrix, tissue, dilation_levels, segment_levels, output_matrix):
    head_dimension = D // HEAD_COUNT
    column_shifts = np.arange(HEAD_COUNT) % DILATION_MIN
    head_sequence = np.arange(HEAD_COUNT)
    key_selected = key_matrix.reshape(GRID_ROWS, GRID_COLUMNS // DILATION_MIN, DILATION_MIN, HEAD_COUNT, head_dimension)[:, :, column_shifts, head_sequence]
    value_selected = value_matrix.reshape(GRID_ROWS, GRID_COLUMNS // DILATION_MIN, DILATION_MIN, HEAD_COUNT, head_dimension)[:, :, column_shifts, head_sequence]
    head_indices = jnp.arange(HEAD_COUNT, dtype=jnp.int32)
    column_indices = jnp.arange(GRID_COLUMNS, dtype=jnp.int32)

    def single_row(row_position):
        q_row = lax.dynamic_index_in_dim(query_matrix, row_position, 0, keepdims=False).reshape(GRID_COLUMNS, HEAD_COUNT, head_dimension).transpose(1, 0, 2)
        k_row = lax.dynamic_index_in_dim(key_selected, row_position, 0, keepdims=False).transpose(1, 0, 2)
        v_row = lax.dynamic_index_in_dim(value_selected, row_position, 0, keepdims=False).transpose(1, 0, 2)
        permitted_mask = dilation_valid_mask(tissue, jnp.full((HEAD_COUNT,), row_position, jnp.int32), head_indices, column_indices, dilation_levels, segment_levels, REACHED_TILES, GRID_COLUMNS)
        softmax_numer, highest, totals = dilation_partial(q_row, k_row, v_row, permitted_mask)
        return (softmax_numer.transpose(1, 0, 2), highest.T, totals.T)
    dilation_numer, dilation_score_max, dilation_sum = lax.map(single_row, jnp.arange(GRID_ROWS, dtype=jnp.int32))
    k_pad = jnp.pad(key_matrix, ((R, R), (R, R), (0, 0)))
    v_pad = jnp.pad(value_matrix, ((R, R), (R, R), (0, 0)))
    tissue_pad = jnp.pad(tissue, R)
    near_both, self_both = window_static(DEVICE_GRID_ROWS, DEVICE_GRID_COLS)
    zero_index = jnp.zeros((), jnp.int32)

    def one_block(block_id):
        row_offset = block_id // N_COL * DEVICE_GRID_ROWS
        column_offset = block_id % N_COL * DEVICE_GRID_COLS
        key_region = lax.dynamic_slice(k_pad, (row_offset, column_offset, zero_index), (DEVICE_GRID_ROWS + 2 * R, DEVICE_GRID_COLS + 2 * R, D)).reshape(-1, D)
        value_region = lax.dynamic_slice(v_pad, (row_offset, column_offset, zero_index), (DEVICE_GRID_ROWS + 2 * R, DEVICE_GRID_COLS + 2 * R, D)).reshape(-1, D)
        tissue_reg = lax.dynamic_slice(tissue_pad, (row_offset, column_offset), (DEVICE_GRID_ROWS + 2 * R, DEVICE_GRID_COLS + 2 * R))
        permitted_mask = jnp.asarray(near_both) & (tissue_reg[None, None] == 1) | jnp.asarray(self_both)
        permitted_mask = permitted_mask.reshape(DEVICE_GRID_ROWS * DEVICE_GRID_COLS, -1)
        queries = lax.dynamic_slice(query_matrix, (row_offset, column_offset, zero_index), (DEVICE_GRID_ROWS, DEVICE_GRID_COLS, D)).reshape(-1, D)
        neighbour_numer, neighbour_max, neighbour_sum = window_part(queries, key_region, value_region, permitted_mask, 2)
        local_block_numer = lax.dynamic_slice(dilation_numer, (row_offset, column_offset, zero_index, zero_index), (DEVICE_GRID_ROWS, DEVICE_GRID_COLS, HEAD_COUNT, head_dimension)).reshape(-1, HEAD_COUNT, head_dimension)
        local_block_max = lax.dynamic_slice(dilation_score_max, (row_offset, column_offset, zero_index), (DEVICE_GRID_ROWS, DEVICE_GRID_COLS, HEAD_COUNT)).reshape(-1, HEAD_COUNT)
        local_block_sum = lax.dynamic_slice(dilation_sum, (row_offset, column_offset, zero_index), (DEVICE_GRID_ROWS, DEVICE_GRID_COLS, HEAD_COUNT)).reshape(-1, HEAD_COUNT)
        attended = merge_partials(neighbour_numer, neighbour_max, neighbour_sum, local_block_numer, local_block_max, local_block_sum).reshape(-1, D).astype(jnp.bfloat16)
        encoded = jnp.dot(attended, output_matrix, preferred_element_type=jnp.float32).astype(jnp.bfloat16)
        return encoded.reshape(DEVICE_GRID_ROWS, DEVICE_GRID_COLS, D)
    blocks = lax.map(one_block, jnp.arange(N_ROW * N_COL, dtype=jnp.int32))
    return blocks.reshape(N_ROW, N_COL, DEVICE_GRID_ROWS, DEVICE_GRID_COLS, D).transpose(0, 2, 1, 3, 4).reshape(GRID_ROWS, GRID_COLUMNS, D)
```

```python
import math

import jax
import jax.numpy as jnp
from jax import lax
from jax.experimental import pallas as pl
from jax.experimental.pallas import tpu as pltpu
from jax.sharding import PartitionSpec as P

HEAD_COUNT = 16
R = 8
STEP = 8
NEG = -1e30
GROUPS = 4
GROUP_HEADS = HEAD_COUNT // GROUPS
WIN = 256
WIN_START = (0, 128, 384, 512)
LOG2E = 1.4426950408889634
STATS = 3


def iota(shape, dim):
    return lax.broadcasted_iota(jnp.int32, shape, dim)


def pack_kernel(q_ref, k_ref, v_ref, send_ref, right_ref, left_ref):
    rows, cols, width = q_ref.shape
    dh = width // HEAD_COUNT
    phase = (iota((STEP, width), 1) // dh) % STEP == iota((STEP, width), 0)
    sub = iota((STEP, width), 0)
    for i, ref in enumerate((k_ref, v_ref)):
        right_ref[i] = ref[:, cols - R :, :]
        left_ref[i] = ref[:, :R, :]
    for r in range(rows):
        tile = jnp.zeros((STEP, width), jnp.float32)
        for i, ref in enumerate((k_ref, v_ref)):
            for j in range(2):
                block = ref[r, j * STEP : (j + 1) * STEP, :].astype(jnp.float32)
                picked = jnp.sum(jnp.where(phase, block, 0.0), axis=0, keepdims=True)
                tile = jnp.where(sub == 2 * i + j, picked, tile)
        tile = tile.astype(jnp.bfloat16)
        for g in range(GROUPS):
            w0 = WIN_START[g]
            send_ref[r * GROUPS + g, :cols, :] = q_ref[r, :, w0 : w0 + WIN]
            send_ref[r * GROUPS + g, cols:, :] = tile[:, w0 : w0 + WIN]


def dilated_kernel(pos_ref, dil_ref, seg_ref, x_ref, tissue_ref, out_ref):
    peers, block_rows, _ = x_ref.shape
    cols = block_rows - STEP
    total_cols = peers * cols
    dh = 48
    group = pos_ref[2]
    odd = group % 2
    keys = peers * STEP
    log_cols = total_cols.bit_length() - 1
    q_all = x_ref[:, :cols, :].reshape(total_cols, WIN)
    kv = x_ref[:, cols:, :].reshape(keys, WIN)
    v_all = pltpu.roll(kv.astype(jnp.float32), keys - 2, 0).astype(jnp.bfloat16)
    lane = iota((1, WIN), 1)
    base = odd * 64
    row = tissue_ref[pl.ds(pos_ref[0], 1), :].astype(jnp.float32)
    row = jnp.broadcast_to(row, (STEP, total_cols)).astype(jnp.bfloat16)
    slot = iota((total_cols, GROUP_HEADS * keys), 1)
    slot_col = (
        ((slot % keys) // STEP) * cols
        + (slot % STEP) * STEP
        + (group * GROUP_HEADS + slot // keys) % STEP
    )
    pick = jnp.where(slot_col == iota((total_cols, GROUP_HEADS * keys), 0), 1.0, 0.0)
    slot_tissue = jnp.dot(row, pick.astype(jnp.bfloat16), preferred_element_type=jnp.float32)[:1]
    key_slot = iota((1, keys), 1)
    query_col = iota((total_cols, 1), 0)
    out = jnp.zeros((total_cols, WIN), jnp.float32)
    stat_base = jnp.where(odd == 1, 0, GROUP_HEADS * dh)
    for hh in range(GROUP_HEADS):
        head = group * GROUP_HEADS + hh
        key_col = (key_slot // STEP) * cols + (key_slot % STEP) * STEP + head % STEP
        period = jnp.left_shift(STEP, dil_ref[head]) - 1
        shift = log_cols - seg_ref[head]
        ok = (key_slot % STEP < 2) & ((key_col & period) == (head & period))
        ok = ok & (slot_tissue[:, hh * keys : (hh + 1) * keys] > 0.5)
        key_seg = jnp.where(ok, jnp.right_shift(key_col, shift), -1)
        mask = key_seg == jnp.right_shift(query_col, shift)
        mine = (lane >= base + hh * dh) & (lane < base + (hh + 1) * dh)
        q_head = jnp.where(mine, q_all, jnp.zeros((), jnp.bfloat16))
        s = lax.dot_general(
            q_head, kv, (((1,), (1,)), ((), ())), preferred_element_type=jnp.float32
        ) * (LOG2E / math.sqrt(dh))
        s = jnp.where(mask, s, NEG)
        top = jnp.max(s, axis=1, keepdims=True)
        p = jnp.where(mask, jnp.exp2(s - top), 0.0)
        total = jnp.sum(p, axis=1, keepdims=True)
        numer = jnp.dot(p.astype(jnp.bfloat16), v_all, preferred_element_type=jnp.float32)
        some = total > 0.0
        safe = jnp.where(some, total, 1.0)
        lse = jnp.where(some, top + jnp.log2(safe), NEG)
        out = jnp.where(mine, numer / safe, out)
        rest = lse
        for part in range(STATS):
            piece = rest.astype(jnp.bfloat16).astype(jnp.float32)
            rest = rest - piece
            out = jnp.where(lane == stat_base + part * GROUP_HEADS + hh, piece, out)
    out_ref[...] = out.astype(jnp.bfloat16).reshape(out_ref.shape)


def window_kernel(pos_ref, q_ref, up_ref, own_ref, down_ref, tissue_ref, out_ref, lse_ref, bias_ref, s_ref, p_ref):
    rows, cols, width = q_ref.shape
    queries = rows * cols
    dh = width // HEAD_COUNT
    wide = cols + 2 * R
    keys = rows * wide
    grid_rows, grid_cols = tissue_ref.shape
    row0, col0 = pos_ref[0], pos_ref[1]
    q_id = iota((queries, keys), 0)
    k_id = iota((queries, keys), 1)
    q_row, q_col = q_id // cols, q_id % cols
    k_row, k_col = k_id // wide, k_id % wide - R
    near_cols = jnp.abs(k_col - q_col) <= R
    spread = jnp.where(iota((grid_cols, keys), 0) == col0 - R + iota((grid_cols, keys), 1) % wide, 1.0, 0.0)
    spread = spread.astype(jnp.bfloat16)
    for b in range(3):
        first = row0 + (b - 1) * rows
        inside = (first >= 0) & (first < grid_rows)
        at = pl.multiple_of(jnp.clip(first, 0, grid_rows - rows), rows)
        tiles = tissue_ref[pl.ds(at, rows), :].astype(jnp.float32).astype(jnp.bfloat16)
        by_row = jnp.dot(tiles, spread, preferred_element_type=jnp.float32)
        mine = iota((rows, keys), 1) // wide == iota((rows, keys), 0)
        flat = jnp.sum(jnp.where(mine, by_row, 0.0), axis=0, keepdims=True)
        live = (flat > 0.5) & inside
        ok = near_cols & (jnp.abs(k_row + (b - 1) * rows - q_row) <= R) & live
        if b == 1:
            ok = ok | ((k_row == q_row) & (k_col == q_col))
        bias_ref[:, b * keys : (b + 1) * keys] = jnp.where(ok, 0.0, NEG)
    lane = iota((1, WIN), 1)
    chunk = 64
    for g in range(GROUPS):
        w0 = WIN_START[g]
        off = g * GROUP_HEADS * dh - w0
        q_win = q_ref[:, :, w0 : w0 + WIN].reshape(queries, WIN)
        stack = []
        for hh in range(GROUP_HEADS):
            mine = (lane >= off + hh * dh) & (lane < off + (hh + 1) * dh)
            stack.append(jnp.where(mine, q_win, jnp.zeros((), jnp.bfloat16)))
        stack = jnp.concatenate(stack, axis=0)
        for b, ref in enumerate((up_ref, own_ref, down_ref)):
            k_win = ref[0, :, :, w0 : w0 + WIN].reshape(keys, WIN)
            s_ref[:, b * keys : (b + 1) * keys] = lax.dot_general(
                stack, k_win, (((1,), (1,)), ((), ())), preferred_element_type=jnp.float32
            )
        tops, totals = [], []
        for c0 in range(0, GROUP_HEADS * queries, chunk):
            b0 = c0 % queries
            s = s_ref[c0 : c0 + chunk, :] * (LOG2E / math.sqrt(dh)) + bias_ref[b0 : b0 + chunk, :]
            top = jnp.max(s, axis=1, keepdims=True)
            p = jnp.exp2(s - top)
            tops.append(top)
            totals.append(jnp.sum(p, axis=1, keepdims=True))
            p_ref[c0 : c0 + chunk, :] = p.astype(jnp.bfloat16)
        numer = jnp.zeros((GROUP_HEADS * queries, WIN), jnp.float32)
        for b, ref in enumerate((up_ref, own_ref, down_ref)):
            v_win = ref[1, :, :, w0 : w0 + WIN].reshape(keys, WIN)
            numer += jnp.dot(
                p_ref[:, b * keys : (b + 1) * keys], v_win, preferred_element_type=jnp.float32
            )
        top = jnp.concatenate(tops, axis=0)
        total = jnp.concatenate(totals, axis=0)
        numer = numer / total
        lse = top + jnp.log2(total)
        out = jnp.zeros((queries, WIN), jnp.float32)
        lse_wide = jnp.zeros((queries, WIN), jnp.float32)
        for hh in range(GROUP_HEADS):
            mine = (lane >= off + hh * dh) & (lane < off + (hh + 1) * dh)
            at = slice(hh * queries, (hh + 1) * queries)
            out = jnp.where(mine, numer[at], out)
            lse_wide = jnp.where(mine, lse[at], lse_wide)
        out_ref[:, g * WIN : (g + 1) * WIN] = out
        lse_ref[:, g * WIN : (g + 1) * WIN] = lse_wide


def merge_kernel(win_ref, lse_ref, back_ref, weight_ref, out_ref):
    rows, cols, width = out_ref.shape
    queries = rows * cols
    dh = width // HEAD_COUNT
    back = back_ref[...].reshape(rows, GROUPS, cols, WIN)
    src = iota((WIN, WIN), 0)
    dst = iota((WIN, WIN), 1)
    pieces = []
    for g in range(GROUPS):
        off = g * GROUP_HEADS * dh - WIN_START[g]
        stat_base = 0 if off else GROUP_HEADS * dh
        x = back[:, g].reshape(queries, WIN)
        stat = src - stat_base
        hit = (stat >= 0) & (stat < STATS * GROUP_HEADS) & (stat % GROUP_HEADS == (dst - off) // dh)
        hit = hit & (dst >= off) & (dst < off + GROUP_HEADS * dh)
        spread = jnp.where(hit, 1.0, 0.0).astype(jnp.bfloat16)
        lse_d = jnp.dot(x, spread, preferred_element_type=jnp.float32)
        lse_w = lse_ref[:, g * WIN : (g + 1) * WIN]
        big = jnp.maximum(lse_w, lse_d)
        a = jnp.exp2(lse_w - big)
        b = jnp.exp2(lse_d - big)
        mixed = a * win_ref[:, g * WIN : (g + 1) * WIN] + b * x.astype(jnp.float32)
        pieces.append(mixed / (a + b))
    low = iota((1, 128), 1) < 64
    att = jnp.concatenate(
        [
            pieces[0][:, :128],
            jnp.where(low, pieces[0][:, 128:], pieces[1][:, :128]),
            pieces[1][:, 128:],
            pieces[2][:, :128],
            jnp.where(low, pieces[2][:, 128:], pieces[3][:, :128]),
            pieces[3][:, 128:],
        ],
        axis=1,
    ).astype(jnp.bfloat16)
    enc = jnp.dot(att, weight_ref[...], preferred_element_type=jnp.float32)
    out_ref[...] = enc.astype(jnp.bfloat16).reshape(out_ref.shape)


def call(kernel, out_shape, scratch=(), scalars=0, inputs=0, flops=0, name=None):
    vmem = pl.BlockSpec(memory_space=pltpu.VMEM)
    smem = pl.BlockSpec(memory_space=pltpu.SMEM)
    many = isinstance(out_shape, (tuple, list))
    return pl.pallas_call(
        kernel,
        out_shape=out_shape,
        in_specs=[smem] * scalars + [vmem] * inputs,
        out_specs=[vmem] * len(out_shape) if many else vmem,
        scratch_shapes=list(scratch),
        cost_estimate=pl.CostEstimate(flops=flops, transcendentals=0, bytes_accessed=1 << 20),
        compiler_params=pltpu.CompilerParams(vmem_limit_bytes=48 << 20),
        name=name,
    )


def per_device(q, k, v, tissue, dilation_levels, segment_levels, weight):
    rows, cols, width = q.shape
    peers = lax.axis_size("col")
    n_row = lax.axis_size("row")
    bf16, f32 = jnp.bfloat16, jnp.float32
    me_row, me_col = lax.axis_index("row"), lax.axis_index("col")
    shape = jax.ShapeDtypeStruct
    half = shape((2, rows, R, width), bf16)
    send, right, left = call(
        pack_kernel,
        [shape((peers, cols + STEP, WIN), bf16), half, half],
        inputs=3,
        name="pack",
    )(q, k, v)
    got = lax.all_to_all(send, "col", 0, 0, tiled=True)
    up_c = [(i, i + 1) for i in range(peers - 1)]
    up_r = [(i, i + 1) for i in range(n_row - 1)]
    from_left = lax.ppermute(right, "col", up_c)
    from_right = lax.ppermute(left, "col", [(b, a) for a, b in up_c])
    own = jnp.concatenate([from_left, jnp.stack([k, v]), from_right], axis=2)
    above = lax.ppermute(own, "row", up_r)
    below = lax.ppermute(own, "row", [(b, a) for a, b in up_r])
    pos_d = jnp.stack([me_row * rows + me_col // GROUPS, me_col * cols, me_col % GROUPS])
    back = call(
        dilated_kernel,
        shape((peers, cols, WIN), bf16),
        scalars=3,
        inputs=2,
        flops=1 << 31,
        name="dilated",
    )(pos_d, dilation_levels, segment_levels, got, tissue)
    back = lax.all_to_all(back, "col", 0, 0, tiled=True)
    keys = rows * (cols + 2 * R)
    queries = rows * cols
    stack = GROUP_HEADS * queries
    win, lse = call(
        window_kernel,
        [shape((queries, GROUPS * WIN), f32)] * 2,
        scratch=[
            pltpu.VMEM((queries, 3 * keys), f32),
            pltpu.VMEM((stack, 3 * keys), f32),
            pltpu.VMEM((stack, 3 * keys), bf16),
        ],
        scalars=1,
        inputs=5,
        flops=1 << 32,
        name="window",
    )(jnp.stack([me_row * rows, me_col * cols]), q, above, own, below, tissue)
    return call(
        merge_kernel, shape((rows, cols, width), bf16), inputs=4, flops=1 << 28, name="merge"
    )(win, lse, back, weight)


def solution(mesh):
    spec = P("row", "col", None)
    return jax.shard_map(
        per_device,
        mesh=mesh,
        in_specs=(spec, spec, spec, P(), P(), P(), P()),
        out_specs=spec,
        check_vma=False,
    )
```

```python
import math

import jax
import jax.numpy as jnp
from jax import lax
from jax.experimental import pallas as pl
from jax.experimental.pallas import tpu as pltpu
from jax.sharding import PartitionSpec as P

HEAD_COUNT = 16
R = 8
STEP = 8
NEG = -1e30
GROUPS = 4
GROUP_HEADS = HEAD_COUNT // GROUPS
WIN = 256
WIN_START = (0, 128, 384, 512)
LOG2E = 1.4426950408889634
STATS = 3


def iota(shape, dim):
    return lax.broadcasted_iota(jnp.int32, shape, dim)


def canonical(x, g):
    full = 3 * (g // 2) + 2 * (g % 2)
    half = 3 * (g // 2) + 1
    return x[:, full * 128 : (full + 1) * 128], x[:, half * 128 : (half + 1) * 128]


def pack_kernel(
    dil_ref, seg_ref, q_hbm, k_hbm, v_hbm, t_hbm, send_ref, right_ref, left_ref, keyseg_ref,
    q_ref, k_ref, v_ref, t_ref, sem,
):
    rows, cols, width = q_ref.shape
    total_cols = t_ref.shape[1]
    dh = width // HEAD_COUNT
    keys = total_cols // cols * STEP
    row0 = pl.multiple_of(lax.axis_index("row") * rows, rows)
    me_col = lax.axis_index("col")
    copies = [
        pltpu.make_async_copy(t_hbm.at[pl.ds(row0, rows), :], t_ref, sem.at[0]),
        pltpu.make_async_copy(k_hbm, k_ref, sem.at[1]),
        pltpu.make_async_copy(v_hbm, v_ref, sem.at[2]),
        pltpu.make_async_copy(q_hbm, q_ref, sem.at[3]),
    ]
    for copy in copies:
        copy.start()
    slot = iota((total_cols, keys), 1)
    pick = (iota((total_cols, keys), 0) == (slot // STEP) * cols + (slot % STEP) * STEP) & (slot % STEP < 2)
    pick = jnp.where(pick, 1.0, 0.0).astype(jnp.bfloat16)
    group = me_col % GROUPS
    sub = iota((STEP, total_cols), 0)
    copies[0].wait()
    tissue = jnp.sum(
        jnp.where(sub == me_col // GROUPS, t_ref[...].astype(jnp.float32), 0.0), axis=0, keepdims=True
    )
    tissue = jnp.broadcast_to(tissue, (STEP, total_cols))
    for bit in range(3):
        shifted = pltpu.roll(tissue, total_cols - (1 << bit), 1)
        tissue = jnp.where(((group * GROUP_HEADS + sub) >> bit) & 1 == 1, shifted, tissue)
    slot_tissue = jnp.dot(tissue.astype(jnp.bfloat16), pick, preferred_element_type=jnp.float32)
    key_slot = iota((1, keys), 1)
    for hh in range(GROUP_HEADS):
        head = group * GROUP_HEADS + hh
        key_col = (key_slot // STEP) * cols + (key_slot % STEP) * STEP + head % STEP
        period = jnp.left_shift(STEP, dil_ref[head]) - 1
        ok = (key_slot % STEP < 2) & ((key_col & period) == (head & period))
        ok = ok & (slot_tissue[hh : hh + 1] > 0.5)
        shift = total_cols.bit_length() - 1 - seg_ref[head]
        keyseg_ref[hh : hh + 1, :] = jnp.where(ok, jnp.right_shift(key_col, shift), -1)
    phase = (iota((STEP, width), 1) // dh) % STEP == iota((STEP, width), 0)
    sub = iota((STEP, width), 0)
    copies[1].wait()
    copies[2].wait()
    tiles = []
    for i, ref in enumerate((k_ref, v_ref)):
        right_ref[i] = ref[:, cols - R :, :]
        left_ref[i] = ref[:, :R, :]
    for r in range(rows):
        tile = jnp.zeros((STEP, width), jnp.float32)
        for i, ref in enumerate((k_ref, v_ref)):
            for j in range(2):
                block = ref[r, j * STEP : (j + 1) * STEP, :].astype(jnp.float32)
                picked = jnp.sum(jnp.where(phase, block, 0.0), axis=0, keepdims=True)
                tile = jnp.where(sub % 4 == 2 * i + j, picked, tile)
        tiles.append(tile)
    copies[3].wait()
    top = iota((STEP, 128), 0) < 4
    low = iota((STEP, 128), 1) < 64
    for r in range(rows):
        for g in range(GROUPS):
            d = r * GROUPS + g
            full, half = canonical(tiles[r], g)
            half = jnp.where(low, pltpu.roll(half, 64, 1) if g % 2 else half, 0.0)
            send_ref[d, 3 * STEP :, :] = jnp.where(top, full, half).astype(jnp.bfloat16)
            full, half = canonical(q_ref[r], g)
            send_ref[d, : 2 * STEP, :] = full
            half = half.astype(jnp.float32)
            first, second = half[:STEP], half[STEP:]
            if g % 2:
                first = pltpu.roll(first, 64, 1)
            else:
                second = pltpu.roll(second, 64, 1)
            send_ref[d, 2 * STEP : 3 * STEP, :] = jnp.where(low, first, second).astype(jnp.bfloat16)


def dilated_kernel(pos_ref, seg_ref, x_ref, keyseg_ref, out_ref, s_ref, p_ref):
    peers = x_ref.shape[0]
    cols = out_ref.shape[1]
    total_cols = peers * cols
    dh = 48
    group = pos_ref[0]
    odd = group % 2
    keys = peers * STEP
    log_cols = total_cols.bit_length() - 1
    low = iota((1, 128), 1) < 64
    zero = jnp.zeros((), jnp.bfloat16)
    q_full = x_ref[:, : 2 * STEP, :].reshape(total_cols, 128)
    packed = x_ref[:, 2 * STEP : 3 * STEP, :].astype(jnp.float32)
    other = pltpu.roll(packed.reshape(peers * STEP, 128), 64, 1).reshape(peers, STEP, 128)
    q_half = jnp.concatenate([packed, other], axis=1).reshape(total_cols, 128)
    q_all = jnp.concatenate([q_full, q_half.astype(jnp.bfloat16)], axis=1)
    kv = x_ref[:, 3 * STEP :, :].astype(jnp.float32).reshape(keys, 128)
    kv2 = pltpu.roll(kv, keys - 2, 0)
    kv4 = pltpu.roll(kv, keys - 4, 0)
    kv6 = pltpu.roll(kv, keys - 6, 0)
    k_all = jnp.concatenate([kv, kv4], axis=1).astype(jnp.bfloat16)
    v_all = jnp.concatenate([kv2, kv6], axis=1).astype(jnp.bfloat16)
    lane = iota((1, WIN), 1)
    place = jnp.where(odd == 1, jnp.where(lane < 128, lane + 64, lane - 128), lane)
    chunk = 128
    out = jnp.zeros((total_cols, WIN), jnp.float32)
    stat = jnp.zeros((total_cols, 128), jnp.float32)
    stat_lane = iota((1, 128), 1)
    for hh in range(GROUP_HEADS):
        mine = (place >= hh * dh) & (place < (hh + 1) * dh) & (lane < 192)
        s_ref[hh * total_cols : (hh + 1) * total_cols, :] = lax.dot_general(
            jnp.where(mine, q_all, zero), k_all, (((1,), (1,)), ((), ())), preferred_element_type=jnp.float32
        )
    for hh in range(GROUP_HEADS):
        mine = (place >= hh * dh) & (place < (hh + 1) * dh) & (lane < 192)
        shift = log_cols - seg_ref[group * GROUP_HEADS + hh]
        keyseg = keyseg_ref[hh : hh + 1, :]
        tops, totals = [], []
        for c0 in range(0, total_cols, chunk):
            bias = jnp.where(keyseg == jnp.right_shift(c0, shift), 0.0, NEG)
            at = slice(hh * total_cols + c0, hh * total_cols + c0 + chunk)
            s = s_ref[at, :] * (LOG2E / math.sqrt(dh)) + bias
            top = jnp.maximum(jnp.max(s, axis=1, keepdims=True), 0.5 * NEG)
            p = jnp.exp2(s - top)
            tops.append(top)
            totals.append(jnp.sum(p, axis=1, keepdims=True))
            p_ref[c0 : c0 + chunk, :] = p.astype(jnp.bfloat16)
        numer = jnp.dot(p_ref[...], v_all, preferred_element_type=jnp.float32)
        total = jnp.concatenate(totals, axis=0)
        safe = jnp.maximum(total, 0.5)
        lse = jnp.where(total > 0.0, jnp.concatenate(tops, axis=0) + jnp.log2(safe), NEG)
        out = jnp.where(mine, numer * (1.0 / safe), out)
        stat = jnp.where(stat_lane % GROUP_HEADS == hh, lse, stat)
    first = stat.astype(jnp.bfloat16).astype(jnp.float32)
    second = (stat - first).astype(jnp.bfloat16).astype(jnp.float32)
    third = stat - first - second
    part = (stat_lane - 64) // GROUP_HEADS
    stat = jnp.where(part == 0, first, jnp.where(part == 1, second, third))
    stat = jnp.where(part < STATS, stat, 0.0)
    out = jnp.concatenate([out[:, :128], jnp.where(low, out[:, 128:], stat)], axis=1)
    out_ref[...] = out.astype(jnp.bfloat16).reshape(out_ref.shape)


def window_kernel(q_ref, up_ref, own_ref, down_ref, tissue_ref, out_ref, lse_ref, bias_ref, s_ref, p_ref):
    rows, cols, width = q_ref.shape
    queries = rows * cols
    dh = width // HEAD_COUNT
    wide = cols + 2 * R
    keys = rows * wide
    grid_rows, grid_cols = tissue_ref.shape
    row0, col0 = lax.axis_index("row") * rows, lax.axis_index("col") * cols
    q_id = iota((queries, keys), 0)
    k_id = iota((queries, keys), 1)
    q_row, q_col = q_id // cols, q_id % cols
    k_row, k_col = k_id // wide, k_id % wide - R
    near_cols = jnp.abs(k_col - q_col) <= R
    spread = jnp.where(iota((grid_cols, keys), 0) == col0 - R + iota((grid_cols, keys), 1) % wide, 1.0, 0.0)
    spread = spread.astype(jnp.bfloat16)
    for b in range(3):
        first = row0 + (b - 1) * rows
        inside = (first >= 0) & (first < grid_rows)
        at = pl.multiple_of(jnp.clip(first, 0, grid_rows - rows), rows)
        tiles = tissue_ref[pl.ds(at, rows), :].astype(jnp.float32).astype(jnp.bfloat16)
        by_row = jnp.dot(tiles, spread, preferred_element_type=jnp.float32)
        mine = iota((rows, keys), 1) // wide == iota((rows, keys), 0)
        flat = jnp.sum(jnp.where(mine, by_row, 0.0), axis=0, keepdims=True)
        live = (flat > 0.5) & inside
        ok = near_cols & (jnp.abs(k_row + (b - 1) * rows - q_row) <= R) & live
        if b == 1:
            ok = ok | ((k_row == q_row) & (k_col == q_col))
        bias_ref[:, b * keys : (b + 1) * keys] = jnp.where(ok, 0.0, NEG)
    lane = iota((1, WIN), 1)
    chunk = 64
    for g in range(GROUPS):
        w0 = WIN_START[g]
        off = g * GROUP_HEADS * dh - w0
        q_win = q_ref[:, :, w0 : w0 + WIN].reshape(queries, WIN)
        stack = []
        for hh in range(GROUP_HEADS):
            mine = (lane >= off + hh * dh) & (lane < off + (hh + 1) * dh)
            stack.append(jnp.where(mine, q_win, jnp.zeros((), jnp.bfloat16)))
        stack = jnp.concatenate(stack, axis=0)
        for b, ref in enumerate((up_ref, own_ref, down_ref)):
            k_win = ref[0, :, :, w0 : w0 + WIN].reshape(keys, WIN)
            s_ref[:, b * keys : (b + 1) * keys] = lax.dot_general(
                stack, k_win, (((1,), (1,)), ((), ())), preferred_element_type=jnp.float32
            )
        tops, totals = [], []
        for c0 in range(0, GROUP_HEADS * queries, chunk):
            b0 = c0 % queries
            s = s_ref[c0 : c0 + chunk, :] * (LOG2E / math.sqrt(dh)) + bias_ref[b0 : b0 + chunk, :]
            top = jnp.max(s, axis=1, keepdims=True)
            p = jnp.exp2(s - top)
            tops.append(top)
            totals.append(jnp.sum(p, axis=1, keepdims=True))
            p_ref[c0 : c0 + chunk, :] = p.astype(jnp.bfloat16)
        numer = jnp.zeros((GROUP_HEADS * queries, WIN), jnp.float32)
        for b, ref in enumerate((up_ref, own_ref, down_ref)):
            v_win = ref[1, :, :, w0 : w0 + WIN].reshape(keys, WIN)
            numer += jnp.dot(
                p_ref[:, b * keys : (b + 1) * keys], v_win, preferred_element_type=jnp.float32
            )
        top = jnp.concatenate(tops, axis=0)
        total = jnp.concatenate(totals, axis=0)
        numer = numer / total
        lse = top + jnp.log2(total)
        out = jnp.zeros((queries, WIN), jnp.float32)
        lse_wide = jnp.zeros((queries, WIN), jnp.float32)
        for hh in range(GROUP_HEADS):
            mine = (lane >= off + hh * dh) & (lane < off + (hh + 1) * dh)
            at = slice(hh * queries, (hh + 1) * queries)
            out = jnp.where(mine, numer[at], out)
            lse_wide = jnp.where(mine, lse[at], lse_wide)
        for ref, wide_block in ((out_ref, out), (lse_ref, lse_wide)):
            if g % 2:
                held = ref[:, w0 : w0 + 128]
                ref[:, w0 : w0 + 128] = jnp.where(iota((1, 128), 1) < 64, held, wide_block[:, :128])
                ref[:, w0 + 128 : w0 + WIN] = wide_block[:, 128:]
            else:
                ref[:, w0 : w0 + WIN] = wide_block


def merge_kernel(win_ref, lse_ref, back_ref, weight_ref, out_ref):
    rows, cols, width = out_ref.shape
    queries = rows * cols
    dh = width // HEAD_COUNT
    back = back_ref[...].reshape(rows, GROUPS, cols, WIN)
    src = iota((WIN, WIN), 0) - 192
    dst = iota((WIN, WIN), 1)
    stat = (src >= 0) & (src < STATS * GROUP_HEADS) & (dst < 192)
    parts = []
    for g in range(GROUPS):
        x = back[:, g].reshape(queries, WIN)
        place = jnp.where(dst < 128, dst + 64, dst - 128) if g % 2 else dst
        spread = jnp.where(stat & (src % GROUP_HEADS == place // dh), 1.0, 0.0).astype(jnp.bfloat16)
        lse_d = jnp.dot(x, spread, preferred_element_type=jnp.float32)
        pair = []
        for y in (x.astype(jnp.float32), lse_d):
            pair.append((y[:, :128], pltpu.roll(y[:, 128:], 64, 1) if g % 2 else y[:, 128:]))
        parts.append(pair)
    low = iota((1, 128), 1) < 64
    att = []
    for tile in range(width // 128):
        pair, place = 2 * (tile // 3), tile % 3
        if place == 1:
            o_d, lse_d = (jnp.where(low, parts[pair][i][1], parts[pair + 1][i][1]) for i in range(2))
        else:
            o_d, lse_d = (parts[pair + place // 2][i][0] for i in range(2))
        at = slice(tile * 128, (tile + 1) * 128)
        lse_w = lse_ref[:, at]
        big = jnp.maximum(lse_w, lse_d)
        a = jnp.exp2(lse_w - big)
        b = jnp.exp2(lse_d - big)
        att.append((a * win_ref[:, at] + b * o_d) / (a + b))
    att = jnp.concatenate(att, axis=1).astype(jnp.bfloat16)
    enc = jnp.dot(att, weight_ref[...], preferred_element_type=jnp.float32)
    out_ref[...] = enc.astype(jnp.bfloat16).reshape(out_ref.shape)


def call(kernel, out_shape, ins, scratch=(), flops=0, name=None):
    spaces = dict(s=pltpu.SMEM, v=pltpu.VMEM, a=pl.ANY)
    vmem = pl.BlockSpec(memory_space=pltpu.VMEM)
    many = isinstance(out_shape, (tuple, list))
    return pl.pallas_call(
        kernel,
        out_shape=out_shape,
        in_specs=[pl.BlockSpec(memory_space=spaces[c]) for c in ins],
        out_specs=[vmem] * len(out_shape) if many else vmem,
        scratch_shapes=list(scratch),
        cost_estimate=pl.CostEstimate(flops=flops, transcendentals=0, bytes_accessed=1 << 20),
        compiler_params=pltpu.CompilerParams(vmem_limit_bytes=20 << 20),
        name=name,
    )


def per_device(q, k, v, tissue, dilation_levels, segment_levels, weight):
    rows, cols, width = q.shape
    peers = lax.axis_size("col")
    n_row = lax.axis_size("row")
    bf16, f32 = jnp.bfloat16, jnp.float32
    shape, vmem = jax.ShapeDtypeStruct, pltpu.VMEM
    keys_d = peers * STEP
    half = shape((2, rows, R, width), bf16)
    send, right, left, keyseg = call(
        pack_kernel,
        [shape((peers, 4 * STEP, 128), bf16), half, half, shape((STEP, keys_d), jnp.int32)],
        ins="ssaaaa",
        scratch=[vmem((rows, cols, width), bf16)] * 3
        + [vmem((rows, tissue.shape[1]), jnp.int32), pltpu.SemaphoreType.DMA((4,))],
        name="pack",
    )(dilation_levels, segment_levels, q, k, v, tissue)
    got = lax.all_to_all(send, "col", 0, 0, tiled=True)
    up_c = [(i, i + 1) for i in range(peers - 1)]
    up_r = [(i, i + 1) for i in range(n_row - 1)]
    from_left = lax.ppermute(right, "col", up_c)
    from_right = lax.ppermute(left, "col", [(b, a) for a, b in up_c])
    own = jnp.concatenate([from_left, jnp.stack([k, v]), from_right], axis=2)
    above = lax.ppermute(own, "row", up_r)
    below = lax.ppermute(own, "row", [(b, a) for a, b in up_r])
    back = call(
        dilated_kernel,
        shape((peers, cols, WIN), bf16),
        ins="ssvv",
        scratch=[vmem((GROUP_HEADS * peers * cols, keys_d), f32), vmem((peers * cols, keys_d), bf16)],
        flops=1 << 31,
        name="dilated",
    )(lax.axis_index("col").reshape(1) % GROUPS, segment_levels, got, keyseg)
    back = lax.all_to_all(back, "col", 0, 0, tiled=True)
    keys = rows * (cols + 2 * R)
    queries = rows * cols
    stack = GROUP_HEADS * queries
    win, lse = call(
        window_kernel,
        [shape((queries, width), f32)] * 2,
        ins="vvvvv",
        scratch=[vmem((queries, 3 * keys), f32), vmem((stack, 3 * keys), f32), vmem((stack, 3 * keys), bf16)],
        flops=1 << 32,
        name="window",
    )(q, above, own, below, tissue)
    return call(merge_kernel, shape((rows, cols, width), bf16), ins="vvvv", flops=1 << 28, name="merge")(
        win, lse, back, weight
    )


def solution(mesh):
    spec = P("row", "col", None)
    return jax.shard_map(
        per_device,
        mesh=mesh,
        in_specs=(spec, spec, spec, P(), P(), P(), P()),
        out_specs=spec,
        check_vma=False,
    )
```

```python
import math

import jax
import jax.numpy as jnp
from jax import lax
from jax.experimental import pallas as pl
from jax.experimental.pallas import tpu as pltpu
from jax.sharding import PartitionSpec as P

HEAD_COUNT = 16
R = 8
STEP = 8
NEG = -1e30
GROUPS = 4
GROUP_HEADS = HEAD_COUNT // GROUPS
WIN = 256
WIN_START = (0, 128, 384, 512)
LOG2E = 1.4426950408889634
CHUNK = 128
STATS = 3


def iota(shape, dim):
    return lax.broadcasted_iota(jnp.int32, shape, dim)


def canonical(x, g):
    full = 3 * (g // 2) + 2 * (g % 2)
    half = 3 * (g // 2) + 1
    return x[:, full * 128 : (full + 1) * 128], x[:, half * 128 : (half + 1) * 128]


def pack_kernel(
    dil_hbm, seg_hbm, q_hbm, k_hbm, v_hbm, t_hbm, send_ref, right_ref, left_ref, bias_ref,
    q_ref, k_ref, v_ref, t_ref, dil_ref, seg_ref, sem,
):
    rows, cols, width = q_ref.shape
    total_cols = t_ref.shape[1]
    dh = width // HEAD_COUNT
    keys = total_cols // cols * STEP
    row0 = pl.multiple_of(lax.axis_index("row") * rows, rows)
    me_col = lax.axis_index("col")
    copies = [
        pltpu.make_async_copy(t_hbm.at[pl.ds(row0, rows), :], t_ref, sem.at[0]),
        pltpu.make_async_copy(k_hbm, k_ref, sem.at[1]),
        pltpu.make_async_copy(v_hbm, v_ref, sem.at[2]),
        pltpu.make_async_copy(q_hbm, q_ref, sem.at[3]),
        pltpu.make_async_copy(dil_hbm, dil_ref, sem.at[4]),
        pltpu.make_async_copy(seg_hbm, seg_ref, sem.at[5]),
    ]
    for copy in copies:
        copy.start()
    slot = iota((total_cols, keys), 1)
    pick = (iota((total_cols, keys), 0) == (slot // STEP) * cols + (slot % STEP) * STEP) & (slot % STEP < 2)
    pick = jnp.where(pick, 1.0, 0.0).astype(jnp.bfloat16)
    group = me_col % GROUPS
    sub = iota((STEP, total_cols), 0)
    copies[0].wait()
    tissue = jnp.sum(
        jnp.where(sub == me_col // GROUPS, t_ref[...].astype(jnp.float32), 0.0), axis=0, keepdims=True
    )
    tissue = jnp.broadcast_to(tissue, (STEP, total_cols))
    for bit in range(3):
        shifted = pltpu.roll(tissue, total_cols - (1 << bit), 1)
        tissue = jnp.where(((group * GROUP_HEADS + sub) >> bit) & 1 == 1, shifted, tissue)
    slot_tissue = jnp.dot(tissue.astype(jnp.bfloat16), pick, preferred_element_type=jnp.float32)
    key_slot = iota((1, keys), 1)
    copies[4].wait()
    copies[5].wait()
    for hh in range(GROUP_HEADS):
        head = group * GROUP_HEADS + hh
        key_col = (key_slot // STEP) * cols + (key_slot % STEP) * STEP + head % STEP
        period = jnp.left_shift(STEP, dil_ref[head]) - 1
        ok = (key_slot % STEP < 2) & ((key_col & period) == (head & period))
        ok = ok & (slot_tissue[hh : hh + 1] > 0.5)
        shift = total_cols.bit_length() - 1 - seg_ref[head]
        key_seg = jnp.where(ok, jnp.right_shift(key_col, shift), -1)
        for c in range(total_cols // CHUNK):
            near = key_seg == jnp.right_shift(c * CHUNK, shift)
            at = hh * (total_cols // CHUNK) + c
            bias_ref[at : at + 1, :] = jnp.where(near, 0.0, NEG)
    phase = (iota((STEP, width), 1) // dh) % STEP == iota((STEP, width), 0)
    sub = iota((STEP, width), 0)
    copies[1].wait()
    copies[2].wait()
    tiles = []
    for i, ref in enumerate((k_ref, v_ref)):
        right_ref[i] = ref[:, cols - R :, :]
        left_ref[i] = ref[:, :R, :]
    for r in range(rows):
        tile = jnp.zeros((STEP, width), jnp.float32)
        for i, ref in enumerate((k_ref, v_ref)):
            for j in range(2):
                block = ref[r, j * STEP : (j + 1) * STEP, :].astype(jnp.float32)
                picked = jnp.sum(jnp.where(phase, block, 0.0), axis=0, keepdims=True)
                tile = jnp.where(sub % 4 == 2 * i + j, picked, tile)
        tiles.append(tile)
    copies[3].wait()
    top = iota((STEP, 128), 0) < 4
    low = iota((STEP, 128), 1) < 64
    for r in range(rows):
        for g in range(GROUPS):
            d = r * GROUPS + g
            full, half = canonical(tiles[r], g)
            half = jnp.where(low, pltpu.roll(half, 64, 1) if g % 2 else half, 0.0)
            send_ref[d, 3 * STEP :, :] = jnp.where(top, full, half).astype(jnp.bfloat16)
            full, half = canonical(q_ref[r], g)
            send_ref[d, : 2 * STEP, :] = full
            half = half.astype(jnp.float32)
            first, second = half[:STEP], half[STEP:]
            if g % 2:
                first = pltpu.roll(first, 64, 1)
            else:
                second = pltpu.roll(second, 64, 1)
            send_ref[d, 2 * STEP : 3 * STEP, :] = jnp.where(low, first, second).astype(jnp.bfloat16)


def dilated_kernel(x_ref, bias_ref, out_ref, s_ref, p_ref):
    peers = x_ref.shape[0]
    cols = out_ref.shape[1]
    total_cols = peers * cols
    dh = 48
    odd = lax.axis_index("col") % 2
    keys = peers * STEP
    low = iota((1, 128), 1) < 64
    zero = jnp.zeros((), jnp.bfloat16)
    q_full = x_ref[:, : 2 * STEP, :].reshape(total_cols, 128)
    packed = x_ref[:, 2 * STEP : 3 * STEP, :].astype(jnp.float32)
    other = pltpu.roll(packed.reshape(peers * STEP, 128), 64, 1).reshape(peers, STEP, 128)
    q_half = jnp.concatenate([packed, other], axis=1).reshape(total_cols, 128)
    q_all = jnp.concatenate([q_full, q_half.astype(jnp.bfloat16)], axis=1)
    kv = x_ref[:, 3 * STEP :, :].astype(jnp.float32).reshape(keys, 128)
    kv2 = pltpu.roll(kv, keys - 2, 0)
    kv4 = pltpu.roll(kv, keys - 4, 0)
    kv6 = pltpu.roll(kv, keys - 6, 0)
    k_all = jnp.concatenate([kv, kv4], axis=1).astype(jnp.bfloat16)
    v_all = jnp.concatenate([kv2, kv6], axis=1).astype(jnp.bfloat16)
    lane = iota((1, WIN), 1)
    place = jnp.where(odd == 1, jnp.where(lane < 128, lane + 64, lane - 128), lane)
    out = jnp.zeros((total_cols, WIN), jnp.float32)
    stat = jnp.zeros((total_cols, 128), jnp.float32)
    stat_lane = iota((1, 128), 1)
    for hh in range(GROUP_HEADS):
        mine = (place >= hh * dh) & (place < (hh + 1) * dh) & (lane < 192)
        s_ref[hh * total_cols : (hh + 1) * total_cols, :] = lax.dot_general(
            jnp.where(mine, q_all, zero), k_all, (((1,), (1,)), ((), ())), preferred_element_type=jnp.float32
        )
    for hh in range(GROUP_HEADS):
        mine = (place >= hh * dh) & (place < (hh + 1) * dh) & (lane < 192)
        tops, totals = [], []
        for c0 in range(0, total_cols, CHUNK):
            row = (hh * total_cols + c0) // CHUNK
            bias = bias_ref[row : row + 1, :]
            at = slice(hh * total_cols + c0, hh * total_cols + c0 + CHUNK)
            s = s_ref[at, :] * (LOG2E / math.sqrt(dh)) + bias
            top = jnp.maximum(jnp.max(s, axis=1, keepdims=True), 0.5 * NEG)
            p = jnp.exp2(s - top)
            tops.append(top)
            totals.append(jnp.sum(p, axis=1, keepdims=True))
            p_ref[c0 : c0 + CHUNK, :] = p.astype(jnp.bfloat16)
        numer = jnp.dot(p_ref[...], v_all, preferred_element_type=jnp.float32)
        total = jnp.concatenate(totals, axis=0)
        safe = jnp.maximum(total, 0.5)
        lse = jnp.where(total > 0.0, jnp.concatenate(tops, axis=0) + jnp.log2(safe), NEG)
        out = jnp.where(mine, numer * (1.0 / safe), out)
        stat = jnp.where(stat_lane % GROUP_HEADS == hh, lse, stat)
    first = stat.astype(jnp.bfloat16).astype(jnp.float32)
    second = (stat - first).astype(jnp.bfloat16).astype(jnp.float32)
    third = stat - first - second
    part = (stat_lane - 64) // GROUP_HEADS
    stat = jnp.where(part == 0, first, jnp.where(part == 1, second, third))
    stat = jnp.where(part < STATS, stat, 0.0)
    out = jnp.concatenate([out[:, :128], jnp.where(low, out[:, 128:], stat)], axis=1)
    out_ref[...] = out.astype(jnp.bfloat16).reshape(out_ref.shape)


def window_kernel(
    q_ref, up_hbm, own_ref, down_hbm, tissue_ref, out_ref, lse_ref, bias_ref, s_ref, p_ref, up_ref, down_ref, sem
):
    copies = [
        pltpu.make_async_copy(up_hbm, up_ref, sem.at[0]),
        pltpu.make_async_copy(down_hbm, down_ref, sem.at[1]),
    ]
    for copy in copies:
        copy.start()
    rows, cols, width = q_ref.shape
    queries = rows * cols
    dh = width // HEAD_COUNT
    wide = cols + 2 * R
    keys = rows * wide
    grid_rows, grid_cols = tissue_ref.shape
    row0, col0 = lax.axis_index("row") * rows, lax.axis_index("col") * cols
    q_id = iota((queries, keys), 0)
    k_id = iota((queries, keys), 1)
    q_row, q_col = q_id // cols, q_id % cols
    k_row, k_col = k_id // wide, k_id % wide - R
    near_cols = jnp.abs(k_col - q_col) <= R
    spread = jnp.where(iota((grid_cols, keys), 0) == col0 - R + iota((grid_cols, keys), 1) % wide, 1.0, 0.0)
    spread = spread.astype(jnp.bfloat16)
    for b in range(3):
        first = row0 + (b - 1) * rows
        inside = (first >= 0) & (first < grid_rows)
        at = pl.multiple_of(jnp.clip(first, 0, grid_rows - rows), rows)
        tiles = tissue_ref[pl.ds(at, rows), :].astype(jnp.float32).astype(jnp.bfloat16)
        by_row = jnp.dot(tiles, spread, preferred_element_type=jnp.float32)
        mine = iota((rows, keys), 1) // wide == iota((rows, keys), 0)
        flat = jnp.sum(jnp.where(mine, by_row, 0.0), axis=0, keepdims=True)
        live = (flat > 0.5) & inside
        ok = near_cols & (jnp.abs(k_row + (b - 1) * rows - q_row) <= R) & live
        if b == 1:
            ok = ok | ((k_row == q_row) & (k_col == q_col))
        bias_ref[:, b * keys : (b + 1) * keys] = jnp.where(ok, 0.0, NEG)
    lane = iota((1, WIN), 1)
    chunk = 64
    for copy in copies:
        copy.wait()
    for g in range(GROUPS):
        w0 = WIN_START[g]
        off = g * GROUP_HEADS * dh - w0
        q_win = q_ref[:, :, w0 : w0 + WIN].reshape(queries, WIN)
        stack = []
        for hh in range(GROUP_HEADS):
            mine = (lane >= off + hh * dh) & (lane < off + (hh + 1) * dh)
            stack.append(jnp.where(mine, q_win, jnp.zeros((), jnp.bfloat16)))
        stack = jnp.concatenate(stack, axis=0)
        for b, ref in enumerate((up_ref, own_ref, down_ref)):
            k_win = ref[0, :, :, w0 : w0 + WIN].reshape(keys, WIN)
            s_ref[:, b * keys : (b + 1) * keys] = lax.dot_general(
                stack, k_win, (((1,), (1,)), ((), ())), preferred_element_type=jnp.float32
            )
        tops, totals = [], []
        for c0 in range(0, GROUP_HEADS * queries, chunk):
            b0 = c0 % queries
            s = s_ref[c0 : c0 + chunk, :] * (LOG2E / math.sqrt(dh)) + bias_ref[b0 : b0 + chunk, :]
            top = jnp.max(s, axis=1, keepdims=True)
            p = jnp.exp2(s - top)
            tops.append(top)
            totals.append(jnp.sum(p, axis=1, keepdims=True))
            p_ref[c0 : c0 + chunk, :] = p.astype(jnp.bfloat16)
        numer = jnp.zeros((GROUP_HEADS * queries, WIN), jnp.float32)
        for b, ref in enumerate((up_ref, own_ref, down_ref)):
            v_win = ref[1, :, :, w0 : w0 + WIN].reshape(keys, WIN)
            numer += jnp.dot(
                p_ref[:, b * keys : (b + 1) * keys], v_win, preferred_element_type=jnp.float32
            )
        top = jnp.concatenate(tops, axis=0)
        total = jnp.concatenate(totals, axis=0)
        numer = numer / total
        lse = top + jnp.log2(total)
        out = jnp.zeros((queries, WIN), jnp.float32)
        lse_wide = jnp.zeros((queries, WIN), jnp.float32)
        for hh in range(GROUP_HEADS):
            mine = (lane >= off + hh * dh) & (lane < off + (hh + 1) * dh)
            at = slice(hh * queries, (hh + 1) * queries)
            out = jnp.where(mine, numer[at], out)
            lse_wide = jnp.where(mine, lse[at], lse_wide)
        for ref, wide_block in ((out_ref, out), (lse_ref, lse_wide)):
            if g % 2:
                held = ref[:, w0 : w0 + 128]
                ref[:, w0 : w0 + 128] = jnp.where(iota((1, 128), 1) < 64, held, wide_block[:, :128])
                ref[:, w0 + 128 : w0 + WIN] = wide_block[:, 128:]
            else:
                ref[:, w0 : w0 + WIN] = wide_block


def merge_kernel(win_ref, lse_ref, back_ref, weight_ref, out_ref):
    rows, cols, width = out_ref.shape
    queries = rows * cols
    dh = width // HEAD_COUNT
    back = back_ref[...].reshape(rows, GROUPS, cols, WIN)
    src = iota((WIN, WIN), 0) - 192
    dst = iota((WIN, WIN), 1)
    stat = (src >= 0) & (src < STATS * GROUP_HEADS) & (dst < 192)
    parts = []
    for g in range(GROUPS):
        x = back[:, g].reshape(queries, WIN)
        place = jnp.where(dst < 128, dst + 64, dst - 128) if g % 2 else dst
        spread = jnp.where(stat & (src % GROUP_HEADS == place // dh), 1.0, 0.0).astype(jnp.bfloat16)
        lse_d = jnp.dot(x, spread, preferred_element_type=jnp.float32)
        pair = []
        for y in (x.astype(jnp.float32), lse_d):
            pair.append((y[:, :128], pltpu.roll(y[:, 128:], 64, 1) if g % 2 else y[:, 128:]))
        parts.append(pair)
    low = iota((1, 128), 1) < 64
    att = []
    for tile in range(width // 128):
        pair, place = 2 * (tile // 3), tile % 3
        if place == 1:
            o_d, lse_d = (jnp.where(low, parts[pair][i][1], parts[pair + 1][i][1]) for i in range(2))
        else:
            o_d, lse_d = (parts[pair + place // 2][i][0] for i in range(2))
        at = slice(tile * 128, (tile + 1) * 128)
        lse_w = lse_ref[:, at]
        big = jnp.maximum(lse_w, lse_d)
        a = jnp.exp2(lse_w - big)
        b = jnp.exp2(lse_d - big)
        att.append((a * win_ref[:, at] + b * o_d) / (a + b))
    att = jnp.concatenate(att, axis=1).astype(jnp.bfloat16)
    enc = jnp.dot(att, weight_ref[...], preferred_element_type=jnp.float32)
    out_ref[...] = enc.astype(jnp.bfloat16).reshape(out_ref.shape)


def call(kernel, out_shape, ins, scratch=(), flops=0, name=None):
    spaces = dict(v=pltpu.VMEM, h=pltpu.HBM)
    vmem = pl.BlockSpec(memory_space=pltpu.VMEM)
    many = isinstance(out_shape, (tuple, list))
    return pl.pallas_call(
        kernel,
        out_shape=out_shape,
        in_specs=[pl.BlockSpec(memory_space=spaces[c]) for c in ins],
        out_specs=[vmem] * len(out_shape) if many else vmem,
        scratch_shapes=list(scratch),
        cost_estimate=pl.CostEstimate(flops=flops, transcendentals=0, bytes_accessed=1 << 20),
        compiler_params=pltpu.CompilerParams(vmem_limit_bytes=20 << 20),
        name=name,
    )


def per_device(q, k, v, tissue, dilation_levels, segment_levels, weight):
    rows, cols, width = q.shape
    peers = lax.axis_size("col")
    n_row = lax.axis_size("row")
    bf16, f32 = jnp.bfloat16, jnp.float32
    shape, vmem = jax.ShapeDtypeStruct, pltpu.VMEM
    keys_d = peers * STEP
    half = shape((2, rows, R, width), bf16)
    hbm = [pltpu.with_memory_space_constraint(x, pltpu.HBM) for x in (dilation_levels, segment_levels, q, k, v, tissue)]
    send, right, left, bias = call(
        pack_kernel,
        [shape((peers, 4 * STEP, 128), bf16), half, half, shape((16, keys_d), f32)],
        ins="hhhhhh",
        scratch=[vmem((rows, cols, width), bf16)] * 3
        + [vmem((rows, tissue.shape[1]), jnp.int32)]
        + [pltpu.SMEM((HEAD_COUNT,), jnp.int32)] * 2
        + [pltpu.SemaphoreType.DMA((6,))],
        name="pack",
    )(*hbm)
    got = lax.all_to_all(send, "col", 0, 0, tiled=True)
    up_c = [(i, i + 1) for i in range(peers - 1)]
    up_r = [(i, i + 1) for i in range(n_row - 1)]
    from_left = lax.ppermute(right, "col", up_c)
    from_right = lax.ppermute(left, "col", [(b, a) for a, b in up_c])
    own = jnp.concatenate([from_left, jnp.stack([k, v]), from_right], axis=2)
    above = lax.ppermute(own, "row", up_r)
    below = lax.ppermute(own, "row", [(b, a) for a, b in up_r])
    back = call(
        dilated_kernel,
        shape((peers, cols, WIN), bf16),
        ins="vv",
        scratch=[vmem((GROUP_HEADS * peers * cols, keys_d), f32), vmem((peers * cols, keys_d), bf16)],
        flops=1 << 31,
        name="dilated",
    )(got, bias)
    back = lax.all_to_all(back, "col", 0, 0, tiled=True)
    keys = rows * (cols + 2 * R)
    queries = rows * cols
    stack = GROUP_HEADS * queries
    win, lse = call(
        window_kernel,
        [shape((queries, width), f32)] * 2,
        ins="vhvhv",
        scratch=[vmem((queries, 3 * keys), f32), vmem((stack, 3 * keys), f32), vmem((stack, 3 * keys), bf16)]
        + [vmem(own.shape, bf16)] * 2
        + [pltpu.SemaphoreType.DMA((2,))],
        flops=1 << 32,
        name="window",
    )(q, pltpu.with_memory_space_constraint(above, pltpu.HBM), own, pltpu.with_memory_space_constraint(below, pltpu.HBM), tissue)
    return call(merge_kernel, shape((rows, cols, width), bf16), ins="vvvv", flops=1 << 28, name="merge")(
        win, lse, back, weight
    )


def solution(mesh):
    spec = P("row", "col", None)
    return jax.shard_map(
        per_device,
        mesh=mesh,
        in_specs=(spec, spec, spec, P(), P(), P(), P()),
        out_specs=spec,
        check_vma=False,
    )
```

```python
import math

import jax
import jax.numpy as jnp
from jax import lax
from jax.experimental import pallas as pl
from jax.experimental.pallas import tpu as pltpu
from jax.sharding import PartitionSpec as P


HEAD_COUNT = 16
R = 8
STEP = 8
NEG = -1e30
GROUPS = 4
GROUP_HEADS = HEAD_COUNT // GROUPS
WIN = 256
WIN_START = (0, 128, 384, 512)
LOG2E = 1.4426950408889634
X = 4
KEYS = 4
SLOTS = 8
STATS = 3


def iota(shape, dim):
    return lax.broadcasted_iota(jnp.int32, shape, dim)


def pack_kernel(
    dil_hbm, seg_hbm, k_hbm, v_hbm, t_hbm, send_ref, right_ref, left_ref, ok_ref,
    k_ref, v_ref, t_ref, dil_ref, seg_ref, sem,
):
    rows, cols, width = k_ref.shape
    total_cols = t_ref.shape[1]
    dh = width // HEAD_COUNT
    slots = total_cols // cols * KEYS
    row0 = pl.multiple_of(lax.axis_index("row") * rows, rows)
    me_col = lax.axis_index("col")
    copies = [
        pltpu.make_async_copy(t_hbm.at[pl.ds(row0, rows), :], t_ref, sem.at[0]),
        pltpu.make_async_copy(k_hbm, k_ref, sem.at[1]),
        pltpu.make_async_copy(v_hbm, v_ref, sem.at[2]),
        pltpu.make_async_copy(dil_hbm, dil_ref, sem.at[3]),
        pltpu.make_async_copy(seg_hbm, seg_ref, sem.at[4]),
    ]
    for copy in copies:
        copy.start()
    slot = iota((total_cols, slots), 1)
    pick = iota((total_cols, slots), 0) == (slot // KEYS) * cols + (slot % 2) * STEP
    pick = jnp.where(pick, 1.0, 0.0).astype(jnp.bfloat16)
    sub = iota((STEP, total_cols), 0)
    copies[0].wait()
    live = []
    for rr in range(2):
        own = jnp.where(sub == me_col % X * 2 + rr, t_ref[...].astype(jnp.float32), 0.0)
        own = jnp.broadcast_to(jnp.sum(own, axis=0, keepdims=True), (STEP, total_cols))
        for bit in range(3):
            own = jnp.where((sub >> bit) & 1 == 1, pltpu.roll(own, total_cols - (1 << bit), 1), own)
        live.append(own)
    live = jnp.concatenate(live, axis=0).astype(jnp.bfloat16)
    live = jnp.dot(live, pick, preferred_element_type=jnp.float32)
    key_slot = iota((STEP, slots), 1)
    key_col = (key_slot // KEYS) * cols + (key_slot % 2) * STEP + iota((STEP, slots), 0)
    phase_id = iota((STEP, slots), 0)
    copies[3].wait()
    copies[4].wait()
    for half in range(HEAD_COUNT // STEP):
        dil = jnp.zeros((STEP, slots), jnp.int32)
        seg = jnp.zeros((STEP, slots), jnp.int32)
        for p in range(STEP):
            dil = jnp.where(phase_id == p, dil_ref[half * STEP + p], dil)
            seg = jnp.where(phase_id == p, seg_ref[half * STEP + p], seg)
        period = jnp.left_shift(STEP, dil) - 1
        shift = total_cols.bit_length() - 1 - seg
        head = phase_id + half * STEP
        ok = (key_col & period) == (head & period)
        ok = ok & (jnp.right_shift(key_col, shift) == jnp.right_shift(me_col // X * (X * cols), shift))
        for rr in range(2):
            good = ok & (key_slot % KEYS // 2 == rr) & (live[rr * STEP : (rr + 1) * STEP] > 0.5)
            at = (half * 2 + rr) * STEP
            ok_ref[at : at + STEP, :] = jnp.where(good, 1.0, 0.0)
    phase = (iota((STEP, width), 1) // dh) % STEP == iota((STEP, width), 0)
    sub = iota((STEP, width), 0)
    copies[1].wait()
    copies[2].wait()
    for i, ref in enumerate((k_ref, v_ref)):
        right_ref[i] = ref[:, cols - R :, :]
        left_ref[i] = ref[:, :R, :]
    for x in range(X):
        tile = jnp.zeros((SLOTS, width), jnp.float32)
        for i, ref in enumerate((k_ref, v_ref)):
            for rr in range(2):
                for j in range(2):
                    block = ref[2 * x + rr, j * STEP : (j + 1) * STEP, :].astype(jnp.float32)
                    picked = jnp.sum(jnp.where(phase, block, 0.0), axis=0, keepdims=True)
                    tile = jnp.where(sub == 4 * i + 2 * rr + j, picked, tile)
        tile = tile.astype(jnp.bfloat16)
        for z in range(send_ref.shape[0] // X):
            send_ref[z * X + x] = tile


NT = (((1,), (1,)), ((), ()))
TN = (((0,), (0,)), ((), ()))


def stacked_queries(q_ref, g):
    rows, cols, width = q_ref.shape
    dh = width // HEAD_COUNT
    w0 = WIN_START[g]
    off = g * GROUP_HEADS * dh - w0
    lane = iota((1, WIN), 1)
    q_win = q_ref[:, :, w0 : w0 + WIN].reshape(rows * cols, WIN)
    zero = jnp.zeros((), jnp.bfloat16)
    first = [off + hh * dh for hh in range(GROUP_HEADS)]
    return jnp.concatenate([jnp.where((lane >= f) & (lane < f + dh), q_win, zero) for f in first], axis=0)


def put_transposed(dst_ref, col, x):
    for tile in range(x.shape[1] // 128):
        part = x[:, tile * 128 : (tile + 1) * 128].astype(jnp.float32)
        dst_ref[tile * 128 : (tile + 1) * 128, col : col + x.shape[0]] = part.T.astype(dst_ref.dtype)


def dilated_kernel(q_ref, kv_ref, ok_ref, out_ref, s_ref, k_ref, vt_ref, ot_ref):
    two_x, cols, width = q_ref.shape
    queries = two_x * cols
    stacked = GROUP_HEADS * queries
    dh = width // HEAD_COUNT
    peers = kv_ref.shape[0]
    upper = iota((SLOTS, width), 0) >= KEYS
    values = []
    for pair in range(peers // 2):
        even = kv_ref[2 * pair].astype(jnp.float32)
        odd = kv_ref[2 * pair + 1].astype(jnp.float32)
        k_ref[pair * SLOTS : (pair + 1) * SLOTS, :] = jnp.where(upper, pltpu.roll(odd, KEYS, 0), even)
        values.append(jnp.where(upper, odd, pltpu.roll(even, KEYS, 0)))
    put_transposed(vt_ref, 0, jnp.concatenate(values, axis=0))
    for g in range(GROUPS):
        w0 = WIN_START[g]
        s_ref[:, g * stacked : (g + 1) * stacked] = lax.dot_general(
            k_ref[:, w0 : w0 + WIN].astype(jnp.bfloat16),
            stacked_queries(q_ref, g),
            NT,
            preferred_element_type=jnp.float32,
        )
    ok = ok_ref[...].astype(jnp.bfloat16)
    part = iota((ok.shape[0], queries), 0)
    odd_row = iota((ok.shape[0], queries), 1) // cols % 2
    lses = []
    for h in range(HEAD_COUNT):
        row = (h // STEP * 2 + odd_row) * STEP + h % STEP
        mine = jnp.where(part == row, 1.0, 0.0).astype(jnp.bfloat16)
        live = lax.dot_general(ok, mine, TN, preferred_element_type=jnp.float32)
        s = s_ref[:, h * queries : (h + 1) * queries] * (LOG2E / math.sqrt(dh))
        s = jnp.where(live > 0.5, s, NEG)
        top = jnp.maximum(jnp.max(s, axis=0, keepdims=True), 0.5 * NEG)
        p = jnp.exp2(s - top)
        total = jnp.sum(p, axis=0, keepdims=True)
        safe = jnp.maximum(total, 0.5)
        numer = jnp.dot(
            vt_ref[h * dh : (h + 1) * dh, :], p.astype(jnp.bfloat16), preferred_element_type=jnp.float32
        )
        ot_ref[h * dh : (h + 1) * dh, :] = numer * (1.0 / safe)
        lses.append(jnp.where(total > 0.0, top + jnp.log2(safe), NEG))
    lse = jnp.concatenate(lses, axis=0)
    first = lse.astype(jnp.bfloat16).astype(jnp.float32)
    second = (lse - first).astype(jnp.bfloat16).astype(jnp.float32)
    for i, piece in enumerate((first, second, lse - first - second)):
        ot_ref[width + i * HEAD_COUNT : width + (i + 1) * HEAD_COUNT, :] = piece
    ot_ref[width + STATS * HEAD_COUNT :, :] = jnp.zeros((128 - STATS * HEAD_COUNT, queries), jnp.float32)
    for tile in range(width // 128 + 1):
        at = slice(tile * 128, (tile + 1) * 128)
        out_ref[:, :, at] = ot_ref[at, :].T.astype(jnp.bfloat16).reshape(two_x, cols, 128)


def window_kernel(
    q_ref, up_hbm, own_ref, down_hbm, tissue_ref, out_ref, top_ref, total_ref,
    bias_ref, s_ref, vt_ref, up_ref, down_ref, sem,
):
    copies = [
        pltpu.make_async_copy(up_hbm, up_ref, sem.at[0]),
        pltpu.make_async_copy(down_hbm, down_ref, sem.at[1]),
    ]
    for copy in copies:
        copy.start()
    rows, cols, width = q_ref.shape
    queries = rows * cols
    stacked = GROUP_HEADS * queries
    dh = width // HEAD_COUNT
    wide = cols + 2 * R
    keys = rows * wide
    grid_rows, grid_cols = tissue_ref.shape
    row0, col0 = lax.axis_index("row") * rows, lax.axis_index("col") * cols
    k_id = iota((keys, queries), 0)
    q_id = iota((keys, queries), 1)
    q_row, q_col = q_id // cols, q_id % cols
    k_row, k_col = k_id // wide, k_id % wide - R
    near_cols = jnp.abs(k_col - q_col) <= R
    lane = iota((grid_cols, 128), 1)
    spread = (iota((grid_cols, 128), 0) == col0 - R + lane) & (lane < wide)
    spread = jnp.where(spread, 1.0, 0.0).astype(jnp.bfloat16)
    by_row = jnp.where(iota((keys, rows), 0) // wide == iota((keys, rows), 1), 1.0, 0.0).astype(jnp.bfloat16)
    own_lane = iota((keys, 128), 1) == iota((keys, 128), 0) % wide
    ones = jnp.ones((128, queries), jnp.bfloat16)
    stacks = [stacked_queries(q_ref, g) for g in range(GROUPS)]
    for b, ref in ((1, own_ref), (0, up_ref), (2, down_ref)):
        at_b = slice(b * keys, (b + 1) * keys)
        first = row0 + (b - 1) * rows
        inside = (first >= 0) & (first < grid_rows)
        at = pl.multiple_of(jnp.clip(first, 0, grid_rows - rows), rows)
        tiles = tissue_ref[pl.ds(at, rows), :].astype(jnp.float32).astype(jnp.bfloat16)
        tiles = jnp.dot(tiles, spread, preferred_element_type=jnp.float32).astype(jnp.bfloat16)
        live = jnp.dot(by_row, tiles, preferred_element_type=jnp.float32)
        live = jnp.where(own_lane, live, 0.0).astype(jnp.bfloat16)
        live = jnp.dot(live, ones, preferred_element_type=jnp.float32)
        ok = near_cols & (jnp.abs(k_row + (b - 1) * rows - q_row) <= R) & (live > 0.5) & inside
        if b == 1:
            ok = ok | ((k_row == q_row) & (k_col == q_col))
        bias_ref[at_b, :] = jnp.where(ok, 0.0, NEG)
        if b == 0:
            for copy in copies:
                copy.wait()
        for g in range(GROUPS):
            w0 = WIN_START[g]
            k_win = ref[0, :, :, w0 : w0 + WIN].reshape(keys, WIN)
            s_ref[at_b, g * stacked : (g + 1) * stacked] = lax.dot_general(
                k_win, stacks[g], NT, preferred_element_type=jnp.float32
            )
        put_transposed(vt_ref, b * keys, ref[1].reshape(keys, width))
    for h in range(HEAD_COUNT):
        s = s_ref[:, h * queries : (h + 1) * queries] * (LOG2E / math.sqrt(dh)) + bias_ref[...]
        top = jnp.max(s, axis=0, keepdims=True)
        p = jnp.exp2(s - top)
        top_ref[h : h + 1, :] = top
        total_ref[h : h + 1, :] = jnp.sum(p, axis=0, keepdims=True)
        out_ref[h * dh : (h + 1) * dh, :] = jnp.dot(
            vt_ref[h * dh : (h + 1) * dh, :], p.astype(jnp.bfloat16), preferred_element_type=jnp.float32
        )


def merge_kernel(win_ref, top_ref, total_ref, back_ref, weight_ref, out_ref, bt_ref, at_ref):
    rows, cols, width = out_ref.shape
    queries = rows * cols
    dh = width // HEAD_COUNT
    put_transposed(bt_ref, 0, back_ref[...].reshape(queries, width + 128))
    lse = bt_ref[width : width + HEAD_COUNT, :]
    for part in range(1, STATS):
        lse = lse + bt_ref[width + part * HEAD_COUNT : width + (part + 1) * HEAD_COUNT, :]
    top = top_ref[...]
    big = jnp.maximum(top, lse)
    a = jnp.exp2(top - big)
    b = jnp.exp2(lse - big)
    inverse = 1.0 / (a * total_ref[...] + b)
    a, b = a * inverse, b * inverse
    for h in range(HEAD_COUNT):
        at = slice(h * dh, (h + 1) * dh)
        mixed = a[h : h + 1] * win_ref[at, :] + b[h : h + 1] * bt_ref[at, :]
        at_ref[at, :] = mixed
    att = jnp.concatenate(
        [at_ref[t * 128 : (t + 1) * 128, :].T.astype(jnp.bfloat16) for t in range(width // 128)], axis=1
    )
    enc = jnp.dot(att, weight_ref[...], preferred_element_type=jnp.float32)
    out_ref[...] = enc.astype(jnp.bfloat16).reshape(out_ref.shape)


def call(kernel, out_shape, ins, scratch=(), flops=0):
    spaces = dict(v=pltpu.VMEM, h=pltpu.HBM)
    vmem = pl.BlockSpec(memory_space=pltpu.VMEM)
    many = isinstance(out_shape, (tuple, list))
    return pl.pallas_call(
        kernel,
        out_shape=out_shape,
        in_specs=[pl.BlockSpec(memory_space=spaces[c]) for c in ins],
        out_specs=[vmem] * len(out_shape) if many else vmem,
        scratch_shapes=list(scratch),
        cost_estimate=pl.CostEstimate(flops=flops, transcendentals=0, bytes_accessed=1 << 20),
        compiler_params=pltpu.CompilerParams(vmem_limit_bytes=24 << 20),
    )


def per_device(q, k, v, tissue, dilation_levels, segment_levels, weight):
    rows, cols, width = q.shape
    peers = lax.axis_size("col")
    n_row = lax.axis_size("row")
    bf16, f32 = jnp.bfloat16, jnp.float32
    shape, vmem = jax.ShapeDtypeStruct, pltpu.VMEM
    slots = peers * KEYS
    x_groups = [[z * X + x for x in range(X)] for z in range(peers // X)]
    half = shape((2, rows, R, width), bf16)
    hbm = [pltpu.with_memory_space_constraint(x, pltpu.HBM) for x in (dilation_levels, segment_levels, k, v, tissue)]
    q_x = lax.all_to_all(q, "col", 0, 0, tiled=True, axis_index_groups=x_groups)
    send, right, left, ok = call(
        pack_kernel,
        [shape((peers, SLOTS, width), bf16), half, half, shape((2 * HEAD_COUNT, slots), f32)],
        ins="hhhhh",
        scratch=[vmem((rows, cols, width), bf16)] * 2
        + [vmem((rows, tissue.shape[1]), jnp.int32)]
        + [pltpu.SMEM((HEAD_COUNT,), jnp.int32)] * 2
        + [pltpu.SemaphoreType.DMA((5,))],
    )(*hbm)
    got = lax.all_to_all(send, "col", 0, 0, tiled=True)
    up_c = [(i, i + 1) for i in range(peers - 1)]
    up_r = [(i, i + 1) for i in range(n_row - 1)]
    from_left = lax.ppermute(right, "col", up_c)
    from_right = lax.ppermute(left, "col", [(b, a) for a, b in up_c])
    own = jnp.concatenate([from_left, jnp.stack([k, v]), from_right], axis=2)
    above = lax.ppermute(own, "row", up_r)
    below = lax.ppermute(own, "row", [(b, a) for a, b in up_r])
    queries = rows * cols
    stack = HEAD_COUNT * queries
    back = call(
        dilated_kernel,
        shape((rows, cols, width + 128), bf16),
        ins="vvv",
        scratch=[
            vmem((slots, stack), f32),
            vmem((slots, width), f32),
            vmem((width, slots), bf16),
            vmem((width + 128, queries), f32),
        ],
        flops=1 << 31,
    )(q_x, got, ok)
    back = lax.all_to_all(back, "col", 0, 0, tiled=True, axis_index_groups=x_groups)
    keys = 3 * rows * (cols + 2 * R)
    above, below = (pltpu.with_memory_space_constraint(x, pltpu.HBM) for x in (above, below))
    per_head = shape((HEAD_COUNT, queries), f32)
    win, top, total = call(
        window_kernel,
        [shape((width, queries), f32), per_head, per_head],
        ins="vhvhv",
        scratch=[vmem((keys, queries), f32), vmem((keys, stack), f32), vmem((width, keys), bf16)]
        + [vmem(own.shape, bf16)] * 2
        + [pltpu.SemaphoreType.DMA((2,))],
        flops=1 << 32,
    )(q, above, own, below, tissue)
    return call(
        merge_kernel,
        shape((rows, cols, width), bf16),
        ins="v" * 5,
        scratch=[vmem((width + 128, queries), f32), vmem((width, queries), f32)],
        flops=1 << 28,
    )(win, top, total, back, weight)


def solution(mesh):
    spec = P("row", "col", None)
    return jax.shard_map(
        per_device,
        mesh=mesh,
        in_specs=(spec, spec, spec, P(), P(), P(), P()),
        out_specs=spec,
        check_vma=False,
    )
```

```python
import functools
import math

import jax
import jax.numpy as jnp
from jax import lax
from jax.experimental import pallas as pl
from jax.experimental.pallas import tpu as pltpu
from jax.sharding import PartitionSpec as P


HEAD_COUNT = 16
R = 8
STEP = 8
NEG = -1e30
GROUPS = 4
GROUP_HEADS = HEAD_COUNT // GROUPS
WIN = 256
WIN_START = (0, 128, 384, 512)
LOG2E = 1.4426950408889634
X = 4
KEYS = 4
SLOTS = 8
STATS = 3


def iota(shape, dim):
    return lax.broadcasted_iota(jnp.int32, shape, dim)


def pack_kernel(
    dil_hbm, seg_hbm, k_hbm, v_hbm, t_hbm, send_ref, right_ref, left_ref, ok_ref,
    k_ref, v_ref, t_ref, dil_ref, seg_ref, sem,
):
    rows, cols, width = k_ref.shape
    total_cols = t_ref.shape[1]
    dh = width // HEAD_COUNT
    slots = total_cols // cols * KEYS
    row0 = pl.multiple_of(lax.axis_index("row") * rows, rows)
    me_col = lax.axis_index("col")
    copies = [
        pltpu.make_async_copy(t_hbm.at[pl.ds(row0, rows), :], t_ref, sem.at[0]),
        pltpu.make_async_copy(k_hbm, k_ref, sem.at[1]),
        pltpu.make_async_copy(v_hbm, v_ref, sem.at[2]),
        pltpu.make_async_copy(dil_hbm, dil_ref, sem.at[3]),
        pltpu.make_async_copy(seg_hbm, seg_ref, sem.at[4]),
    ]
    for copy in copies:
        copy.start()
    slot = iota((total_cols, slots), 1)
    pick = iota((total_cols, slots), 0) == (slot // KEYS) * cols + (slot % 2) * STEP
    pick = jnp.where(pick, 1.0, 0.0).astype(jnp.bfloat16)
    sub = iota((STEP, total_cols), 0)
    copies[0].wait()
    live = []
    for rr in range(2):
        own = jnp.where(sub == me_col % X * 2 + rr, t_ref[...].astype(jnp.float32), 0.0)
        own = jnp.broadcast_to(jnp.sum(own, axis=0, keepdims=True), (STEP, total_cols))
        for bit in range(3):
            own = jnp.where((sub >> bit) & 1 == 1, pltpu.roll(own, total_cols - (1 << bit), 1), own)
        live.append(own)
    live = jnp.concatenate(live, axis=0).astype(jnp.bfloat16)
    live = jnp.dot(live, pick, preferred_element_type=jnp.float32)
    ok_ref[...] = jnp.zeros(ok_ref.shape, jnp.float32)
    key_slot = iota((STEP, slots), 1)
    key_col = (key_slot // KEYS) * cols + (key_slot % 2) * STEP + iota((STEP, slots), 0)
    phase_id = iota((STEP, slots), 0)
    copies[3].wait()
    copies[4].wait()
    for half in range(HEAD_COUNT // STEP):
        dil = jnp.zeros((STEP, slots), jnp.int32)
        seg = jnp.zeros((STEP, slots), jnp.int32)
        for p in range(STEP):
            dil = jnp.where(phase_id == p, dil_ref[half * STEP + p], dil)
            seg = jnp.where(phase_id == p, seg_ref[half * STEP + p], seg)
        period = jnp.left_shift(STEP, dil) - 1
        shift = total_cols.bit_length() - 1 - seg
        head = phase_id + half * STEP
        ok = (key_col & period) == (head & period)
        ok = ok & (jnp.right_shift(key_col, shift) == jnp.right_shift(me_col // X * (X * cols), shift))
        for rr in range(2):
            good = ok & (key_slot % KEYS // 2 == rr) & (live[rr * STEP : (rr + 1) * STEP] > 0.5)
            at = (half * 2 + rr) * STEP
            for copy_at in (at, at + 64):
                ok_ref[copy_at : copy_at + STEP, :] = jnp.where(good, 0.0, NEG)
    phase = (iota((STEP, width), 1) // dh) % STEP == iota((STEP, width), 0)
    sub = iota((STEP, width), 0)
    copies[1].wait()
    copies[2].wait()
    for i, ref in enumerate((k_ref, v_ref)):
        right_ref[i] = ref[:, cols - R :, :]
        left_ref[i] = ref[:, :R, :]
    for x in range(X):
        tile = jnp.zeros((SLOTS, width), jnp.float32)
        for i, ref in enumerate((k_ref, v_ref)):
            for rr in range(2):
                for j in range(2):
                    block = ref[2 * x + rr, j * STEP : (j + 1) * STEP, :].astype(jnp.float32)
                    picked = jnp.sum(jnp.where(phase, block, 0.0), axis=0, keepdims=True)
                    tile = jnp.where(sub == 4 * i + 2 * rr + j, picked, tile)
        tile = tile.astype(jnp.bfloat16)
        for z in range(send_ref.shape[0] // X):
            send_ref[z * X + x] = tile


NT = (((1,), (1,)), ((), ()))


def stacked_queries(q_ref, g):
    rows, cols, width = q_ref.shape
    dh = width // HEAD_COUNT
    w0 = WIN_START[g]
    off = g * GROUP_HEADS * dh - w0
    lane = iota((1, WIN), 1)
    q_win = q_ref[:, :, w0 : w0 + WIN].reshape(rows * cols, WIN)
    zero = jnp.zeros((), jnp.bfloat16)
    first = [off + hh * dh for hh in range(GROUP_HEADS)]
    return jnp.concatenate([jnp.where((lane >= f) & (lane < f + dh), q_win, zero) for f in first], axis=0)


def put_transposed(dst_ref, col, x):
    for tile in range(x.shape[1] // 128):
        part = x[:, tile * 128 : (tile + 1) * 128].astype(jnp.float32)
        dst_ref[tile * 128 : (tile + 1) * 128, col : col + x.shape[0]] = part.T.astype(dst_ref.dtype)


def dilated_kernel(q_ref, kv_ref, ok_ref, out_ref, s_ref, k_ref, vt_ref, ot_ref):
    two_x, cols, width = q_ref.shape
    queries = two_x * cols
    stacked = GROUP_HEADS * queries
    dh = width // HEAD_COUNT
    peers = kv_ref.shape[0]
    upper = iota((SLOTS, width), 0) >= KEYS
    values = []
    for pair in range(peers // 2):
        even = kv_ref[2 * pair].astype(jnp.float32)
        odd = kv_ref[2 * pair + 1].astype(jnp.float32)
        k_ref[pair * SLOTS : (pair + 1) * SLOTS, :] = jnp.where(upper, pltpu.roll(odd, KEYS, 0), even)
        values.append(jnp.where(upper, odd, pltpu.roll(even, KEYS, 0)))
    put_transposed(vt_ref, 0, jnp.concatenate(values, axis=0))
    penalty = ok_ref[...].T.astype(jnp.bfloat16)
    lane = iota((1, 128), 1)
    q_id = iota((stacked, 128), 0)
    for g in range(GROUPS):
        w0 = WIN_START[g]
        head = g * GROUP_HEADS + q_id // queries
        row = (head // STEP * 2 + q_id // cols % 2) * STEP + head % STEP
        choose = jnp.where(lane % 64 == row, 1.0, 0.0).astype(jnp.bfloat16)
        stack = stacked_queries(q_ref, g)
        k_win = k_ref[:, w0 : w0 + WIN].astype(jnp.bfloat16)
        if g % 2:
            stack = jnp.concatenate([jnp.where(lane < 64, choose, stack[:, :128]), stack[:, 128:]], axis=1)
            k_win = jnp.concatenate([jnp.where(lane < 64, penalty, k_win[:, :128]), k_win[:, 128:]], axis=1)
        else:
            stack = jnp.concatenate([stack[:, :128], jnp.where(lane < 64, stack[:, 128:], choose)], axis=1)
            k_win = jnp.concatenate([k_win[:, :128], jnp.where(lane < 64, k_win[:, 128:], penalty)], axis=1)
        s_ref[:, g * stacked : (g + 1) * stacked] = lax.dot_general(
            k_win, stack, NT, preferred_element_type=jnp.float32
        )
    lses = []
    for g in range(GROUPS):
        s = s_ref[:, g * stacked : (g + 1) * stacked] * (LOG2E / math.sqrt(dh))
        top = jnp.maximum(jnp.max(s, axis=0, keepdims=True), 0.1 * NEG)
        p = jnp.exp2(s - top)
        total = jnp.sum(p, axis=0, keepdims=True)
        p = p.astype(jnp.bfloat16)
        safe = jnp.maximum(total, 0.5)
        lse = jnp.where(total > 0.0, top + jnp.log2(safe), NEG)
        inverse = 1.0 / safe
        for hh in range(GROUP_HEADS):
            h = g * GROUP_HEADS + hh
            at = slice(hh * queries, (hh + 1) * queries)
            numer = jnp.dot(vt_ref[h * dh : (h + 1) * dh, :], p[:, at], preferred_element_type=jnp.float32)
            ot_ref[h * dh : (h + 1) * dh, :] = numer * inverse[:, at]
            lses.append(lse[:, at])
    lse = jnp.concatenate(lses, axis=0)
    first = lse.astype(jnp.bfloat16).astype(jnp.float32)
    second = (lse - first).astype(jnp.bfloat16).astype(jnp.float32)
    for i, piece in enumerate((first, second, lse - first - second)):
        ot_ref[width + i * HEAD_COUNT : width + (i + 1) * HEAD_COUNT, :] = piece
    ot_ref[width + STATS * HEAD_COUNT :, :] = jnp.zeros((128 - STATS * HEAD_COUNT, queries), jnp.float32)
    for tile in range(width // 128 + 1):
        at = slice(tile * 128, (tile + 1) * 128)
        out_ref[:, :, at] = ot_ref[at, :].T.astype(jnp.bfloat16).reshape(two_x, cols, 128)


def window_kernel(*refs, blocks):
    n = len(blocks)
    q_ref, tissue_ref = refs[:2]
    sources = refs[2 : 2 + n]
    out_ref, top_ref, total_ref, bias_ref, s_ref, vt_ref = refs[2 + n : 8 + n]
    copies = []
    if len(refs) > 8 + n:
        held = refs[8 + n : -1]
        copies = [pltpu.make_async_copy(sources[i], held[i], refs[-1].at[i]) for i in range(n)]
        sources = held
    for copy in copies:
        copy.start()
    rows, cols, width = q_ref.shape
    queries = rows * cols
    stacked = GROUP_HEADS * queries
    dh = width // HEAD_COUNT
    wide = cols + 2 * R
    keys = rows * wide
    grid_rows, grid_cols = tissue_ref.shape
    row0, col0 = lax.axis_index("row") * rows, lax.axis_index("col") * cols
    k_id = iota((keys, queries), 0)
    q_id = iota((keys, queries), 1)
    q_row, q_col = q_id // cols, q_id % cols
    k_row, k_col = k_id // wide, k_id % wide - R
    near_cols = jnp.abs(k_col - q_col) <= R
    lane = iota((grid_cols, 128), 1)
    spread = (iota((grid_cols, 128), 0) == col0 - R + lane) & (lane < wide)
    spread = jnp.where(spread, 1.0, 0.0).astype(jnp.bfloat16)
    by_row = jnp.where(iota((keys, rows), 0) // wide == iota((keys, rows), 1), 1.0, 0.0).astype(jnp.bfloat16)
    own_lane = iota((keys, 128), 1) == iota((keys, 128), 0) % wide
    ones = jnp.ones((128, queries), jnp.bfloat16)
    stacks = [stacked_queries(q_ref, g) for g in range(GROUPS)]
    for i, (b, ref) in enumerate(zip(blocks, sources, strict=True)):
        at_b = slice(i * keys, (i + 1) * keys)
        first = row0 + b * rows
        inside = (first >= 0) & (first < grid_rows)
        at = pl.multiple_of(jnp.clip(first, 0, grid_rows - rows), rows)
        tiles = tissue_ref[pl.ds(at, rows), :].astype(jnp.float32).astype(jnp.bfloat16)
        tiles = jnp.dot(tiles, spread, preferred_element_type=jnp.float32).astype(jnp.bfloat16)
        live = jnp.dot(by_row, tiles, preferred_element_type=jnp.float32)
        live = jnp.where(own_lane, live, 0.0).astype(jnp.bfloat16)
        live = jnp.dot(live, ones, preferred_element_type=jnp.float32)
        ok = near_cols & (jnp.abs(k_row + b * rows - q_row) <= R) & (live > 0.5) & inside
        if b == 0:
            ok = ok | ((k_row == q_row) & (k_col == q_col))
        bias_ref[at_b, :] = jnp.where(ok, 0.0, NEG)
        if copies:
            copies[i].wait()
        for g in range(GROUPS):
            w0 = WIN_START[g]
            k_win = ref[0, :, :, w0 : w0 + WIN].reshape(keys, WIN)
            s_ref[at_b, g * stacked : (g + 1) * stacked] = lax.dot_general(
                k_win, stacks[g], NT, preferred_element_type=jnp.float32
            )
        put_transposed(vt_ref, i * keys, ref[1].reshape(keys, width))
    for h in range(HEAD_COUNT):
        s = s_ref[:, h * queries : (h + 1) * queries] * (LOG2E / math.sqrt(dh)) + bias_ref[...]
        top = jnp.maximum(jnp.max(s, axis=0, keepdims=True), 0.1 * NEG)
        p = jnp.exp2(s - top)
        top_ref[h : h + 1, :] = top
        total_ref[h : h + 1, :] = jnp.sum(p, axis=0, keepdims=True)
        out_ref[h * dh : (h + 1) * dh, :] = jnp.dot(
            vt_ref[h * dh : (h + 1) * dh, :], p.astype(jnp.bfloat16), preferred_element_type=jnp.float32
        )


def merge_kernel(
    own_ref, own_top_ref, own_total_ref, far_ref, far_top_ref, far_total_ref, back_ref, weight_ref, out_ref,
    bt_ref, at_ref,
):
    rows, cols, width = out_ref.shape
    queries = rows * cols
    dh = width // HEAD_COUNT
    put_transposed(bt_ref, 0, back_ref[...].reshape(queries, width + 128))
    lse = bt_ref[width : width + HEAD_COUNT, :]
    for part in range(1, STATS):
        lse = lse + bt_ref[width + part * HEAD_COUNT : width + (part + 1) * HEAD_COUNT, :]
    big = jnp.maximum(jnp.maximum(own_top_ref[...], far_top_ref[...]), lse)
    a = jnp.exp2(own_top_ref[...] - big)
    b = jnp.exp2(far_top_ref[...] - big)
    c = jnp.exp2(lse - big)
    inverse = 1.0 / (a * own_total_ref[...] + b * far_total_ref[...] + c)
    a, b, c = a * inverse, b * inverse, c * inverse
    for h in range(HEAD_COUNT):
        at = slice(h * dh, (h + 1) * dh)
        one = slice(h, h + 1)
        at_ref[at, :] = a[one] * own_ref[at, :] + b[one] * far_ref[at, :] + c[one] * bt_ref[at, :]
    att = jnp.concatenate(
        [at_ref[t * 128 : (t + 1) * 128, :].T.astype(jnp.bfloat16) for t in range(width // 128)], axis=1
    )
    enc = jnp.dot(att, weight_ref[...], preferred_element_type=jnp.float32)
    out_ref[...] = enc.astype(jnp.bfloat16).reshape(out_ref.shape)


def call(kernel, out_shape, ins, scratch=(), flops=0):
    spaces = dict(v=pltpu.VMEM, h=pltpu.HBM)
    vmem = pl.BlockSpec(memory_space=pltpu.VMEM)
    many = isinstance(out_shape, (tuple, list))
    return pl.pallas_call(
        kernel,
        out_shape=out_shape,
        in_specs=[pl.BlockSpec(memory_space=spaces[c]) for c in ins],
        out_specs=[vmem] * len(out_shape) if many else vmem,
        scratch_shapes=list(scratch),
        cost_estimate=pl.CostEstimate(flops=flops, transcendentals=0, bytes_accessed=1 << 20),
        compiler_params=pltpu.CompilerParams(vmem_limit_bytes=24 << 20),
    )


def per_device(q, k, v, tissue, dilation_levels, segment_levels, weight):
    rows, cols, width = q.shape
    peers = lax.axis_size("col")
    n_row = lax.axis_size("row")
    bf16, f32 = jnp.bfloat16, jnp.float32
    shape, vmem = jax.ShapeDtypeStruct, pltpu.VMEM
    slots = peers * KEYS
    x_groups = [[z * X + x for x in range(X)] for z in range(peers // X)]
    half = shape((2, rows, R, width), bf16)
    hbm = [pltpu.with_memory_space_constraint(x, pltpu.HBM) for x in (dilation_levels, segment_levels, k, v, tissue)]
    q_x = lax.all_to_all(q, "col", 0, 0, tiled=True, axis_index_groups=x_groups)
    send, right, left, ok = call(
        pack_kernel,
        [shape((peers, SLOTS, width), bf16), half, half, shape((128, slots), f32)],
        ins="hhhhh",
        scratch=[vmem((rows, cols, width), bf16)] * 2
        + [vmem((rows, tissue.shape[1]), jnp.int32)]
        + [pltpu.SMEM((HEAD_COUNT,), jnp.int32)] * 2
        + [pltpu.SemaphoreType.DMA((5,))],
    )(*hbm)
    got = lax.all_to_all(send, "col", 0, 0, tiled=True)
    up_c = [(i, i + 1) for i in range(peers - 1)]
    up_r = [(i, i + 1) for i in range(n_row - 1)]
    from_left = lax.ppermute(right, "col", up_c)
    from_right = lax.ppermute(left, "col", [(b, a) for a, b in up_c])
    own = jnp.concatenate([from_left, jnp.stack([k, v]), from_right], axis=2)
    above = lax.ppermute(own, "row", up_r)
    below = lax.ppermute(own, "row", [(b, a) for a, b in up_r])
    queries = rows * cols
    stack = HEAD_COUNT * queries
    back = call(
        dilated_kernel,
        shape((rows, cols, width + 128), bf16),
        ins="vvv",
        scratch=[
            vmem((slots, stack), f32),
            vmem((slots, width), f32),
            vmem((width, slots), bf16),
            vmem((width + 128, queries), f32),
        ],
        flops=1 << 31,
    )(q_x, got, ok)
    back = lax.all_to_all(back, "col", 0, 0, tiled=True, axis_index_groups=x_groups)
    keys = rows * (cols + 2 * R)
    per_head = shape((HEAD_COUNT, queries), f32)

    def window(blocks, sources, ins, extra=()):
        n = len(blocks) * keys
        return call(
            functools.partial(window_kernel, blocks=blocks),
            [shape((width, queries), f32), per_head, per_head],
            ins="vv" + ins,
            scratch=[vmem((n, queries), f32), vmem((n, stack), f32), vmem((width, n), bf16), *extra],
            flops=len(blocks) << 31,
        )(q, tissue, *sources)

    own_parts = window((0,), (own,), "v")
    above, below = (pltpu.with_memory_space_constraint(x, pltpu.HBM) for x in (above, below))
    extra = [vmem(own.shape, bf16)] * 2 + [pltpu.SemaphoreType.DMA((2,))]
    far_parts = window((-1, 1), (above, below), "hh", extra)
    return call(
        merge_kernel,
        shape((rows, cols, width), bf16),
        ins="v" * 8,
        scratch=[vmem((width + 128, queries), f32), vmem((width, queries), f32)],
        flops=1 << 28,
    )(*own_parts, *far_parts, back, weight)


def solution(mesh):
    spec = P("row", "col", None)
    return jax.shard_map(
        per_device,
        mesh=mesh,
        in_specs=(spec, spec, spec, P(), P(), P(), P()),
        out_specs=spec,
        check_vma=False,
    )
```

```python
import functools
import math

import jax
import jax.numpy as jnp
from jax import lax
from jax.experimental import pallas as pl
from jax.experimental.pallas import tpu as pltpu
from jax.sharding import PartitionSpec as P


HEAD_COUNT = 16
R = 8
STEP = 8
NEG = -1e30
GROUPS = 4
GROUP_HEADS = HEAD_COUNT // GROUPS
WIN = 256
WIN_START = (0, 128, 384, 512)
LOG2E = 1.4426950408889634
X = 4
KEYS = 4
SLOTS = 8
STATS = 3


def iota(shape, dim):
    return lax.broadcasted_iota(jnp.int32, shape, dim)


def pack_kernel(
    dil_hbm, seg_hbm, k_hbm, v_hbm, t_hbm, q_hbm, send_ref, right_ref, left_ref, ok_ref,
    k_ref, v_ref, t_ref, dil_ref, seg_ref, q_ref, tile_ref, sem,
):
    rows, cols, width = k_ref.shape
    total_cols = t_ref.shape[1]
    dh = width // HEAD_COUNT
    slots = total_cols // cols * KEYS
    row0 = pl.multiple_of(lax.axis_index("row") * rows, rows)
    me_col = lax.axis_index("col")
    copies = [
        pltpu.make_async_copy(t_hbm.at[pl.ds(row0, rows), :], t_ref, sem.at[0]),
        pltpu.make_async_copy(k_hbm, k_ref, sem.at[1]),
        pltpu.make_async_copy(v_hbm, v_ref, sem.at[2]),
        pltpu.make_async_copy(dil_hbm, dil_ref, sem.at[3]),
        pltpu.make_async_copy(seg_hbm, seg_ref, sem.at[4]),
    ]
    queries = q_hbm.shape[1]
    copies += [
        pltpu.make_async_copy(q_hbm, q_ref, sem.at[5]),
    ]
    for copy in copies:
        copy.start()
    slot = iota((total_cols, slots), 1)
    pick = iota((total_cols, slots), 0) == (slot // KEYS) * cols + (slot % 2) * STEP
    pick = jnp.where(pick, 1.0, 0.0).astype(jnp.bfloat16)
    sub = iota((STEP, total_cols), 0)
    copies[0].wait()
    live = []
    for rr in range(2):
        own = jnp.where(sub == me_col % X * 2 + rr, t_ref[...].astype(jnp.float32), 0.0)
        own = jnp.broadcast_to(jnp.sum(own, axis=0, keepdims=True), (STEP, total_cols))
        for bit in range(3):
            own = jnp.where((sub >> bit) & 1 == 1, pltpu.roll(own, total_cols - (1 << bit), 1), own)
        live.append(own)
    live = jnp.concatenate(live, axis=0).astype(jnp.bfloat16)
    live = jnp.dot(live, pick, preferred_element_type=jnp.float32)
    ok_ref[...] = jnp.zeros(ok_ref.shape, jnp.float32)
    key_slot = iota((STEP, slots), 1)
    key_col = (key_slot // KEYS) * cols + (key_slot % 2) * STEP + iota((STEP, slots), 0)
    phase_id = iota((STEP, slots), 0)
    copies[3].wait()
    copies[4].wait()
    for half in range(HEAD_COUNT // STEP):
        dil = jnp.zeros((STEP, slots), jnp.int32)
        seg = jnp.zeros((STEP, slots), jnp.int32)
        for p in range(STEP):
            dil = jnp.where(phase_id == p, dil_ref[half * STEP + p], dil)
            seg = jnp.where(phase_id == p, seg_ref[half * STEP + p], seg)
        period = jnp.left_shift(STEP, dil) - 1
        shift = total_cols.bit_length() - 1 - seg
        head = phase_id + half * STEP
        ok = (key_col & period) == (head & period)
        ok = ok & (jnp.right_shift(key_col, shift) == jnp.right_shift(me_col // X * (X * cols), shift))
        for rr in range(2):
            good = ok & (key_slot % KEYS // 2 == rr) & (live[rr * STEP : (rr + 1) * STEP] > 0.5)
            at = (half * 2 + rr) * STEP
            for copy_at in (at, at + 64):
                ok_ref[copy_at : copy_at + STEP, :] = jnp.where(good, 0.0, NEG)
    phase = (iota((STEP, width), 1) // dh) % STEP == iota((STEP, width), 0)
    sub = iota((STEP, width), 0)
    copies[1].wait()
    copies[2].wait()
    for i, ref in enumerate((k_ref, v_ref)):
        right_ref[i] = ref[:, cols - R :, :]
        left_ref[i] = ref[:, :R, :]
    for x in range(X):
        tile = jnp.zeros((SLOTS, width), jnp.float32)
        for i, ref in enumerate((k_ref, v_ref)):
            for rr in range(2):
                for j in range(2):
                    block = ref[2 * x + rr, j * STEP : (j + 1) * STEP, :].astype(jnp.float32)
                    picked = jnp.sum(jnp.where(phase, block, 0.0), axis=0, keepdims=True)
                    tile = jnp.where(sub == 4 * i + 2 * rr + j, picked, tile)
        tile_ref[x] = tile.astype(jnp.bfloat16)
        if x == 0:
            copies[5].wait()
            sends = [pltpu.make_async_copy(q_ref, send_ref.at[:, pl.ds(0, queries), :], sem.at[6])]
            sends[0].start()
    sends.append(pltpu.make_async_copy(tile_ref, send_ref.at[:, pl.ds(queries, SLOTS), :], sem.at[7]))
    sends[1].start()
    for copy in sends:
        copy.wait()


NT = (((1,), (1,)), ((), ()))


def stacked_queries(q_ref, g, take):
    rows, cols, width = q_ref.shape[0], take, q_ref.shape[2]
    dh = width // HEAD_COUNT
    w0 = WIN_START[g]
    off = g * GROUP_HEADS * dh - w0
    lane = iota((1, WIN), 1)
    q_win = q_ref[:, :take, w0 : w0 + WIN].reshape(rows * cols, WIN)
    zero = jnp.zeros((), jnp.bfloat16)
    first = [off + hh * dh for hh in range(GROUP_HEADS)]
    return jnp.concatenate([jnp.where((lane >= f) & (lane < f + dh), q_win, zero) for f in first], axis=0)


def put_transposed(dst_ref, col, x):
    for tile in range(x.shape[1] // 128):
        part = x[:, tile * 128 : (tile + 1) * 128].astype(jnp.float32)
        dst_ref[tile * 128 : (tile + 1) * 128, col : col + x.shape[0]] = part.T.astype(dst_ref.dtype)


def dilated_kernel(q_ref, kv_ref, ok_ref, out_ref, s_ref, k_ref, vt_ref, ot_ref):
    two_x, cols, width = out_ref.shape[0], out_ref.shape[1], q_ref.shape[2]
    queries = two_x * cols
    stacked = GROUP_HEADS * queries
    dh = width // HEAD_COUNT
    peers = kv_ref.shape[0]
    upper = iota((SLOTS, width), 0) >= KEYS
    values = []
    for pair in range(peers // 2):
        even = kv_ref[2 * pair].astype(jnp.float32)
        odd = kv_ref[2 * pair + 1].astype(jnp.float32)
        k_ref[pair * SLOTS : (pair + 1) * SLOTS, :] = jnp.where(upper, pltpu.roll(odd, KEYS, 0), even)
        values.append(jnp.where(upper, odd, pltpu.roll(even, KEYS, 0)))
    put_transposed(vt_ref, 0, jnp.concatenate(values, axis=0))
    penalty = ok_ref[...].T.astype(jnp.bfloat16)
    lane = iota((1, 128), 1)
    second = iota((queries, 128), 0) // cols % 2 == 1
    for g in range(GROUPS):
        w0 = WIN_START[g]
        choose = []
        for head in range(g * GROUP_HEADS, (g + 1) * GROUP_HEADS):
            row = head // STEP * 2 * STEP + head % STEP
            one = (jnp.where(lane % 64 == row + rr * STEP, 1.0, 0.0) for rr in range(2))
            zero, one = (jnp.broadcast_to(x, (queries, 128)) for x in one)
            choose.append(jnp.where(second, one, zero).astype(jnp.bfloat16))
        choose = jnp.concatenate(choose, axis=0)
        stack = stacked_queries(q_ref, g, 2 * cols)
        k_win = k_ref[:, w0 : w0 + WIN].astype(jnp.bfloat16)
        if g % 2:
            stack = jnp.concatenate([jnp.where(lane < 64, choose, stack[:, :128]), stack[:, 128:]], axis=1)
            k_win = jnp.concatenate([jnp.where(lane < 64, penalty, k_win[:, :128]), k_win[:, 128:]], axis=1)
        else:
            stack = jnp.concatenate([stack[:, :128], jnp.where(lane < 64, stack[:, 128:], choose)], axis=1)
            k_win = jnp.concatenate([k_win[:, :128], jnp.where(lane < 64, k_win[:, 128:], penalty)], axis=1)
        s_ref[:, g * stacked : (g + 1) * stacked] = lax.dot_general(
            k_win, stack, NT, preferred_element_type=jnp.float32
        )
    lses = []
    for g in range(GROUPS):
        s = s_ref[:, g * stacked : (g + 1) * stacked] * (LOG2E / math.sqrt(dh))
        top = jnp.maximum(jnp.max(s, axis=0, keepdims=True), 0.1 * NEG)
        p = jnp.exp2(s - top)
        total = jnp.sum(p, axis=0, keepdims=True)
        p = p.astype(jnp.bfloat16)
        safe = jnp.maximum(total, 0.5)
        lse = jnp.where(total > 0.0, top + jnp.log2(safe), NEG)
        inverse = 1.0 / safe
        for hh in range(GROUP_HEADS):
            h = g * GROUP_HEADS + hh
            at = slice(hh * queries, (hh + 1) * queries)
            numer = jnp.dot(vt_ref[h * dh : (h + 1) * dh, :], p[:, at], preferred_element_type=jnp.float32)
            ot_ref[h * dh : (h + 1) * dh, :] = numer * inverse[:, at]
            lses.append(lse[:, at])
    lse = jnp.concatenate(lses, axis=0)
    first = lse.astype(jnp.bfloat16).astype(jnp.float32)
    second = (lse - first).astype(jnp.bfloat16).astype(jnp.float32)
    for i, piece in enumerate((first, second, lse - first - second)):
        ot_ref[width + i * HEAD_COUNT : width + (i + 1) * HEAD_COUNT, :] = piece
    ot_ref[width + STATS * HEAD_COUNT :, :] = jnp.zeros((128 - STATS * HEAD_COUNT, queries), jnp.float32)
    for tile in range(width // 128 + 1):
        at = slice(tile * 128, (tile + 1) * 128)
        out_ref[:, :, at] = ot_ref[at, :].T.astype(jnp.bfloat16).reshape(two_x, cols, 128)


def window_kernel(*refs, blocks):
    n = len(blocks)
    q_ref, tissue_ref = refs[:2]
    sources = refs[2 : 2 + n]
    out_ref, top_ref, total_ref, bias_ref, s_ref, vt_ref = refs[2 + n : 8 + n]
    copies = []
    if len(refs) > 8 + n:
        held = refs[8 + n : -1]
        copies = [pltpu.make_async_copy(sources[i], held[i], refs[-1].at[i]) for i in range(n)]
        sources = held
    for copy in copies:
        copy.start()
    rows, cols, width = q_ref.shape
    queries = rows * cols
    stacked = GROUP_HEADS * queries
    dh = width // HEAD_COUNT
    wide = cols + 2 * R
    keys = rows * wide
    grid_rows, grid_cols = tissue_ref.shape
    row0, col0 = lax.axis_index("row") * rows, lax.axis_index("col") * cols
    k_id = iota((keys, queries), 0)
    q_id = iota((keys, queries), 1)
    q_row, q_col = q_id // cols, q_id % cols
    k_row, k_col = k_id // wide, k_id % wide - R
    near_cols = jnp.abs(k_col - q_col) <= R
    lane = iota((grid_cols, 128), 1)
    spread = (iota((grid_cols, 128), 0) == col0 - R + lane) & (lane < wide)
    spread = jnp.where(spread, 1.0, 0.0).astype(jnp.bfloat16)
    by_row = jnp.where(iota((keys, rows), 0) // wide == iota((keys, rows), 1), 1.0, 0.0).astype(jnp.bfloat16)
    own_lane = iota((keys, 128), 1) == iota((keys, 128), 0) % wide
    ones = jnp.ones((128, queries), jnp.bfloat16)
    stacks = [stacked_queries(q_ref, g, cols) for g in range(GROUPS)]
    for i, (b, ref) in enumerate(zip(blocks, sources, strict=True)):
        at_b = slice(i * keys, (i + 1) * keys)
        first = row0 + b * rows
        inside = (first >= 0) & (first < grid_rows)
        at = pl.multiple_of(jnp.clip(first, 0, grid_rows - rows), rows)
        tiles = tissue_ref[pl.ds(at, rows), :].astype(jnp.float32).astype(jnp.bfloat16)
        tiles = jnp.dot(tiles, spread, preferred_element_type=jnp.float32).astype(jnp.bfloat16)
        live = jnp.dot(by_row, tiles, preferred_element_type=jnp.float32)
        live = jnp.where(own_lane, live, 0.0).astype(jnp.bfloat16)
        live = jnp.dot(live, ones, preferred_element_type=jnp.float32)
        ok = near_cols & (jnp.abs(k_row + b * rows - q_row) <= R) & (live > 0.5) & inside
        if b == 0:
            ok = ok | ((k_row == q_row) & (k_col == q_col))
        bias_ref[at_b, :] = jnp.where(ok, 0.0, NEG)
        if copies:
            copies[i].wait()
        for g in range(GROUPS):
            w0 = WIN_START[g]
            k_win = ref[0, :, :, w0 : w0 + WIN].reshape(keys, WIN)
            s_ref[at_b, g * stacked : (g + 1) * stacked] = lax.dot_general(
                k_win, stacks[g], NT, preferred_element_type=jnp.float32
            )
        put_transposed(vt_ref, i * keys, ref[1].reshape(keys, width))
    for h in range(HEAD_COUNT):
        s = s_ref[:, h * queries : (h + 1) * queries] * (LOG2E / math.sqrt(dh)) + bias_ref[...]
        top = jnp.maximum(jnp.max(s, axis=0, keepdims=True), 0.1 * NEG)
        p = jnp.exp2(s - top)
        top_ref[h : h + 1, :] = top
        total_ref[h : h + 1, :] = jnp.sum(p, axis=0, keepdims=True)
        out_ref[h * dh : (h + 1) * dh, :] = jnp.dot(
            vt_ref[h * dh : (h + 1) * dh, :], p.astype(jnp.bfloat16), preferred_element_type=jnp.float32
        )


def merge_kernel(
    own_ref, own_top_ref, own_total_ref, far_ref, far_top_ref, far_total_ref, back_ref, weight_ref, out_ref,
    bt_ref, at_ref,
):
    rows, cols, width = out_ref.shape
    queries = rows * cols
    dh = width // HEAD_COUNT
    put_transposed(bt_ref, 0, back_ref[...].reshape(queries, width + 128))
    lse = bt_ref[width : width + HEAD_COUNT, :]
    for part in range(1, STATS):
        lse = lse + bt_ref[width + part * HEAD_COUNT : width + (part + 1) * HEAD_COUNT, :]
    big = jnp.maximum(jnp.maximum(own_top_ref[...], far_top_ref[...]), lse)
    a = jnp.exp2(own_top_ref[...] - big)
    b = jnp.exp2(far_top_ref[...] - big)
    c = jnp.exp2(lse - big)
    inverse = 1.0 / (a * own_total_ref[...] + b * far_total_ref[...] + c)
    a, b, c = a * inverse, b * inverse, c * inverse
    for h in range(HEAD_COUNT):
        at = slice(h * dh, (h + 1) * dh)
        one = slice(h, h + 1)
        at_ref[at, :] = a[one] * own_ref[at, :] + b[one] * far_ref[at, :] + c[one] * bt_ref[at, :]
    att = jnp.concatenate(
        [at_ref[t * 128 : (t + 1) * 128, :].T.astype(jnp.bfloat16) for t in range(width // 128)], axis=1
    )
    enc = jnp.dot(att, weight_ref[...], preferred_element_type=jnp.float32)
    out_ref[...] = enc.astype(jnp.bfloat16).reshape(out_ref.shape)


def call(kernel, out_shape, ins, scratch=(), flops=0, outs=None):
    spaces = dict(v=pltpu.VMEM, h=pltpu.HBM)
    many = isinstance(out_shape, (tuple, list))
    return pl.pallas_call(
        kernel,
        out_shape=out_shape,
        in_specs=[pl.BlockSpec(memory_space=spaces[c]) for c in ins],
        out_specs=[pl.BlockSpec(memory_space=spaces[c]) for c in outs or "v" * len(out_shape)]
        if many
        else pl.BlockSpec(memory_space=pltpu.VMEM),
        scratch_shapes=list(scratch),
        cost_estimate=pl.CostEstimate(flops=flops, transcendentals=0, bytes_accessed=1 << 20),
        compiler_params=pltpu.CompilerParams(vmem_limit_bytes=24 << 20),
    )


def per_device(q, k, v, tissue, dilation_levels, segment_levels, weight):
    rows, cols, width = q.shape
    peers = lax.axis_size("col")
    n_row = lax.axis_size("row")
    bf16, f32 = jnp.bfloat16, jnp.float32
    shape, vmem = jax.ShapeDtypeStruct, pltpu.VMEM
    slots = peers * KEYS
    x_groups = [[z * X + x for x in range(X)] for z in range(peers // X)]
    half = shape((2, rows, R, width), bf16)
    hbm = [pltpu.with_memory_space_constraint(x, pltpu.HBM) for x in (dilation_levels, segment_levels, k, v, tissue)]
    hbm.append(pltpu.with_memory_space_constraint(q.reshape(X, 2 * cols, width), pltpu.HBM))
    send, right, left, ok = call(
        pack_kernel,
        [shape((X, 2 * cols + SLOTS, width), bf16), half, half, shape((128, slots), f32)],
        ins="hhhhhh",
        outs="hvvv",
        scratch=[vmem((rows, cols, width), bf16)] * 2
        + [vmem((rows, tissue.shape[1]), jnp.int32)]
        + [pltpu.SMEM((HEAD_COUNT,), jnp.int32)] * 2
        + [vmem((X, 2 * cols, width), bf16), vmem((X, SLOTS, width), bf16), pltpu.SemaphoreType.DMA((8,))],
    )(*hbm)
    stripe = lax.all_to_all(send, "col", 0, 0, tiled=True, axis_index_groups=x_groups)
    z_groups = [[z * X + x for z in range(peers // X)] for x in range(X)]
    got = jnp.broadcast_to(stripe[None, :, 2 * cols :], (peers // X, X, SLOTS, width))
    got = lax.all_to_all(got.reshape(peers, SLOTS, width), "col", 0, 0, tiled=True, axis_index_groups=z_groups)
    up_c = [(i, i + 1) for i in range(peers - 1)]
    up_r = [(i, i + 1) for i in range(n_row - 1)]
    from_left = lax.ppermute(right, "col", up_c)
    from_right = lax.ppermute(left, "col", [(b, a) for a, b in up_c])
    own = jnp.concatenate([from_left, jnp.stack([k, v]), from_right], axis=2)
    above = lax.ppermute(own, "row", up_r)
    below = lax.ppermute(own, "row", [(b, a) for a, b in up_r])
    queries = rows * cols
    stack = HEAD_COUNT * queries
    back = call(
        dilated_kernel,
        shape((rows, cols, width + 128), bf16),
        ins="vvv",
        scratch=[
            vmem((slots, stack), f32),
            vmem((slots, width), f32),
            vmem((width, slots), bf16),
            vmem((width + 128, queries), f32),
        ],
        flops=1 << 31,
    )(stripe, got, ok)
    back = lax.all_to_all(back, "col", 0, 0, tiled=True, axis_index_groups=x_groups)
    keys = rows * (cols + 2 * R)
    per_head = shape((HEAD_COUNT, queries), f32)

    def window(blocks, sources, ins, extra=()):
        n = len(blocks) * keys
        return call(
            functools.partial(window_kernel, blocks=blocks),
            [shape((width, queries), f32), per_head, per_head],
            ins="vv" + ins,
            scratch=[vmem((n, queries), f32), vmem((n, stack), f32), vmem((width, n), bf16), *extra],
            flops=len(blocks) << 31,
        )(q, tissue, *sources)

    own_parts = window((0,), (own,), "v")
    above, below = (pltpu.with_memory_space_constraint(x, pltpu.HBM) for x in (above, below))
    extra = [vmem(own.shape, bf16)] * 2 + [pltpu.SemaphoreType.DMA((2,))]
    far_parts = window((-1, 1), (above, below), "hh", extra)
    return call(
        merge_kernel,
        shape((rows, cols, width), bf16),
        ins="v" * 8,
        scratch=[vmem((width + 128, queries), f32), vmem((width, queries), f32)],
        flops=1 << 28,
    )(*own_parts, *far_parts, back, weight)


def solution(mesh):
    spec = P("row", "col", None)
    return jax.shard_map(
        per_device,
        mesh=mesh,
        in_specs=(spec, spec, spec, P(), P(), P(), P()),
        out_specs=spec,
        check_vma=False,
    )
```

```python
import functools
import math

import jax
import jax.numpy as jnp
from jax import lax
from jax.experimental import pallas as pl
from jax.experimental.pallas import tpu as pltpu
from jax.sharding import PartitionSpec as P


HEAD_COUNT = 16
R = 8
STEP = 8
NEG = -1e30
GROUPS = 4
GROUP_HEADS = HEAD_COUNT // GROUPS
WIN = 256
WIN_START = (0, 128, 384, 512)
LOG2E = 1.4426950408889634
X = 4
KEYS = 4
SLOTS = 8
STATS = 3


def iota(shape, dim):
    return lax.broadcasted_iota(jnp.int32, shape, dim)


def pack_kernel(
    dil_hbm, seg_hbm, k_hbm, v_hbm, t_hbm, q_hbm, send_ref, first_ref, second_ref, ok_ref,
    k_ref, v_ref, t_ref, dil_ref, seg_ref, q_ref, tile_ref, sem,
):
    rows, cols, width = k_ref.shape
    total_cols = t_ref.shape[1]
    dh = width // HEAD_COUNT
    slots = total_cols // cols * KEYS
    row0 = pl.multiple_of(lax.axis_index("row") * rows, rows)
    me_col = lax.axis_index("col")
    copies = [
        pltpu.make_async_copy(t_hbm.at[pl.ds(row0, rows), :], t_ref, sem.at[0]),
        pltpu.make_async_copy(k_hbm, k_ref, sem.at[1]),
        pltpu.make_async_copy(v_hbm, v_ref, sem.at[2]),
        pltpu.make_async_copy(dil_hbm, dil_ref, sem.at[3]),
        pltpu.make_async_copy(seg_hbm, seg_ref, sem.at[4]),
    ]
    queries = q_hbm.shape[1]
    copies += [
        pltpu.make_async_copy(q_hbm, q_ref, sem.at[5]),
    ]
    for copy in copies:
        copy.start()
    slot = iota((total_cols, slots), 1)
    pick = iota((total_cols, slots), 0) == (slot // KEYS) * cols + (slot % 2) * STEP
    pick = jnp.where(pick, 1.0, 0.0).astype(jnp.bfloat16)
    sub = iota((STEP, total_cols), 0)
    copies[0].wait()
    live = []
    for rr in range(2):
        own = jnp.where(sub == me_col % X * 2 + rr, t_ref[...].astype(jnp.float32), 0.0)
        own = jnp.broadcast_to(jnp.sum(own, axis=0, keepdims=True), (STEP, total_cols))
        for bit in range(3):
            own = jnp.where((sub >> bit) & 1 == 1, pltpu.roll(own, total_cols - (1 << bit), 1), own)
        live.append(own)
    live = jnp.concatenate(live, axis=0).astype(jnp.bfloat16)
    live = jnp.dot(live, pick, preferred_element_type=jnp.float32)
    ok_ref[...] = jnp.zeros(ok_ref.shape, jnp.float32)
    key_slot = iota((STEP, slots), 1)
    key_col = (key_slot // KEYS) * cols + (key_slot % 2) * STEP + iota((STEP, slots), 0)
    phase_id = iota((STEP, slots), 0)
    copies[3].wait()
    copies[4].wait()
    for half in range(HEAD_COUNT // STEP):
        dil = jnp.zeros((STEP, slots), jnp.int32)
        seg = jnp.zeros((STEP, slots), jnp.int32)
        for p in range(STEP):
            dil = jnp.where(phase_id == p, dil_ref[half * STEP + p], dil)
            seg = jnp.where(phase_id == p, seg_ref[half * STEP + p], seg)
        period = jnp.left_shift(STEP, dil) - 1
        shift = total_cols.bit_length() - 1 - seg
        head = phase_id + half * STEP
        ok = (key_col & period) == (head & period)
        ok = ok & (jnp.right_shift(key_col, shift) == jnp.right_shift(me_col // X * (X * cols), shift))
        for rr in range(2):
            good = ok & (key_slot % KEYS // 2 == rr) & (live[rr * STEP : (rr + 1) * STEP] > 0.5)
            at = (half * 2 + rr) * STEP
            for copy_at in (at, at + 64):
                ok_ref[copy_at : copy_at + STEP, :] = jnp.where(good, 0.0, NEG)
    phase = (iota((STEP, width), 1) // dh) % STEP == iota((STEP, width), 0)
    sub = iota((STEP, width), 0)
    copies[1].wait()
    copies[2].wait()
    for x in range(X):
        tile = jnp.zeros((SLOTS, width), jnp.float32)
        for i, ref in enumerate((k_ref, v_ref)):
            for rr in range(2):
                for j in range(2):
                    block = ref[2 * x + rr, j * STEP : (j + 1) * STEP, :].astype(jnp.float32)
                    picked = jnp.sum(jnp.where(phase, block, 0.0), axis=0, keepdims=True)
                    tile = jnp.where(sub == 4 * i + 2 * rr + j, picked, tile)
        tile_ref[x] = tile.astype(jnp.bfloat16)
        if x == 0:
            copies[5].wait()
            sends = [pltpu.make_async_copy(q_ref, send_ref.at[:, pl.ds(0, queries), :], sem.at[6])]
            sends[0].start()
    sends.append(pltpu.make_async_copy(tile_ref, send_ref.at[:, pl.ds(queries, SLOTS), :], sem.at[7]))
    sends[1].start()
    for i, ref in enumerate((k_ref, v_ref)):
        right, left = ref[:, cols - R :, :], ref[:, :R, :]
        first_ref[i] = jnp.where(me_col % 2 == 0, right, left)
        second_ref[i] = jnp.where(me_col % 2 == 0, left, right)
    for copy in sends:
        copy.wait()


NT = (((1,), (1,)), ((), ()))


def stacked_queries(q_ref, g, take):
    rows, cols, width = q_ref.shape[0], take, q_ref.shape[2]
    dh = width // HEAD_COUNT
    w0 = WIN_START[g]
    off = g * GROUP_HEADS * dh - w0
    lane = iota((1, WIN), 1)
    q_win = q_ref[:, :take, w0 : w0 + WIN].reshape(rows * cols, WIN)
    zero = jnp.zeros((), jnp.bfloat16)
    first = [off + hh * dh for hh in range(GROUP_HEADS)]
    return jnp.concatenate([jnp.where((lane >= f) & (lane < f + dh), q_win, zero) for f in first], axis=0)


def put_transposed(dst_ref, col, x):
    for tile in range(x.shape[1] // 128):
        part = x[:, tile * 128 : (tile + 1) * 128].astype(jnp.float32)
        dst_ref[tile * 128 : (tile + 1) * 128, col : col + x.shape[0]] = part.T.astype(dst_ref.dtype)


def dilated_kernel(q_ref, kv_ref, ok_ref, out_ref, s_ref, k_ref, vt_ref, ot_ref):
    two_x, cols, width = out_ref.shape[0], out_ref.shape[1], q_ref.shape[2]
    queries = two_x * cols
    stacked = GROUP_HEADS * queries
    dh = width // HEAD_COUNT
    peers = kv_ref.shape[0]
    upper = iota((SLOTS, width), 0) >= KEYS
    values = []
    for pair in range(peers // 2):
        even = kv_ref[2 * pair].astype(jnp.float32)
        odd = kv_ref[2 * pair + 1].astype(jnp.float32)
        k_ref[pair * SLOTS : (pair + 1) * SLOTS, :] = jnp.where(upper, pltpu.roll(odd, KEYS, 0), even)
        values.append(jnp.where(upper, odd, pltpu.roll(even, KEYS, 0)))
    put_transposed(vt_ref, 0, jnp.concatenate(values, axis=0))
    penalty = ok_ref[...].T.astype(jnp.bfloat16)
    lane = iota((1, 128), 1)
    second = iota((queries, 128), 0) // cols % 2 == 1
    for g in range(GROUPS):
        w0 = WIN_START[g]
        choose = []
        for head in range(g * GROUP_HEADS, (g + 1) * GROUP_HEADS):
            row = head // STEP * 2 * STEP + head % STEP
            one = (jnp.where(lane % 64 == row + rr * STEP, 1.0, 0.0) for rr in range(2))
            zero, one = (jnp.broadcast_to(x, (queries, 128)) for x in one)
            choose.append(jnp.where(second, one, zero).astype(jnp.bfloat16))
        choose = jnp.concatenate(choose, axis=0)
        stack = stacked_queries(q_ref, g, 2 * cols)
        k_win = k_ref[:, w0 : w0 + WIN].astype(jnp.bfloat16)
        if g % 2:
            stack = jnp.concatenate([jnp.where(lane < 64, choose, stack[:, :128]), stack[:, 128:]], axis=1)
            k_win = jnp.concatenate([jnp.where(lane < 64, penalty, k_win[:, :128]), k_win[:, 128:]], axis=1)
        else:
            stack = jnp.concatenate([stack[:, :128], jnp.where(lane < 64, stack[:, 128:], choose)], axis=1)
            k_win = jnp.concatenate([k_win[:, :128], jnp.where(lane < 64, k_win[:, 128:], penalty)], axis=1)
        s_ref[:, g * stacked : (g + 1) * stacked] = lax.dot_general(
            k_win, stack, NT, preferred_element_type=jnp.float32
        )
    lses = []
    for g in range(GROUPS):
        s = s_ref[:, g * stacked : (g + 1) * stacked] * (LOG2E / math.sqrt(dh))
        top = jnp.maximum(jnp.max(s, axis=0, keepdims=True), 0.1 * NEG)
        p = jnp.exp2(s - top)
        total = jnp.sum(p, axis=0, keepdims=True)
        p = p.astype(jnp.bfloat16)
        safe = jnp.maximum(total, 0.5)
        lse = jnp.where(total > 0.0, top + jnp.log2(safe), NEG)
        inverse = 1.0 / safe
        for hh in range(GROUP_HEADS):
            h = g * GROUP_HEADS + hh
            at = slice(hh * queries, (hh + 1) * queries)
            numer = jnp.dot(vt_ref[h * dh : (h + 1) * dh, :], p[:, at], preferred_element_type=jnp.float32)
            ot_ref[h * dh : (h + 1) * dh, :] = numer * inverse[:, at]
            lses.append(lse[:, at])
    lse = jnp.concatenate(lses, axis=0)
    first = lse.astype(jnp.bfloat16).astype(jnp.float32)
    second = (lse - first).astype(jnp.bfloat16).astype(jnp.float32)
    for i, piece in enumerate((first, second, lse - first - second)):
        ot_ref[width + i * HEAD_COUNT : width + (i + 1) * HEAD_COUNT, :] = piece
    ot_ref[width + STATS * HEAD_COUNT :, :] = jnp.zeros((128 - STATS * HEAD_COUNT, queries), jnp.float32)
    for tile in range(width // 128 + 1):
        at = slice(tile * 128, (tile + 1) * 128)
        out_ref[:, :, at] = ot_ref[at, :].T.astype(jnp.bfloat16).reshape(two_x, cols, 128)


def window_kernel(*refs, blocks):
    n = len(blocks)
    q_ref, tissue_ref = refs[:2]
    sources = refs[2 : 2 + n]
    out_ref, top_ref, total_ref, bias_ref, s_ref, vt_ref = refs[2 + n : 8 + n]
    copies = []
    if len(refs) > 8 + n:
        held = refs[8 + n : -1]
        copies = [pltpu.make_async_copy(sources[i], held[i], refs[-1].at[i]) for i in range(n)]
        sources = held
    for copy in copies:
        copy.start()
    rows, cols, width = q_ref.shape
    queries = rows * cols
    stacked = GROUP_HEADS * queries
    dh = width // HEAD_COUNT
    wide = cols + 2 * R
    keys = rows * wide
    grid_rows, grid_cols = tissue_ref.shape
    row0, col0 = lax.axis_index("row") * rows, lax.axis_index("col") * cols
    k_id = iota((keys, queries), 0)
    q_id = iota((keys, queries), 1)
    q_row, q_col = q_id // cols, q_id % cols
    turn = lax.axis_index("col") % 2 * (wide - R)

    def column(at):
        return at - R + jnp.where(at < R, turn, 0) - jnp.where(at >= wide - R, turn, 0)

    side = 1 - lax.axis_index("row") % 2 * 2
    k_row, k_col = k_id // wide, column(k_id % wide)
    near_cols = jnp.abs(k_col - q_col) <= R
    lane = iota((grid_cols, 128), 1)
    spread = (iota((grid_cols, 128), 0) == col0 + column(lane)) & (lane < wide)
    spread = jnp.where(spread, 1.0, 0.0).astype(jnp.bfloat16)
    by_row = jnp.where(iota((keys, rows), 0) // wide == iota((keys, rows), 1), 1.0, 0.0).astype(jnp.bfloat16)
    own_lane = iota((keys, 128), 1) == iota((keys, 128), 0) % wide
    ones = jnp.ones((128, queries), jnp.bfloat16)
    stacks = [stacked_queries(q_ref, g, cols) for g in range(GROUPS)]
    for i, (b, ref) in enumerate(zip(blocks, sources, strict=True)):
        at_b = slice(i * keys, (i + 1) * keys)
        b = b * side
        first = row0 + b * rows
        inside = (first >= 0) & (first < grid_rows)
        at = pl.multiple_of(jnp.clip(first, 0, grid_rows - rows), rows)
        tiles = tissue_ref[pl.ds(at, rows), :].astype(jnp.float32).astype(jnp.bfloat16)
        tiles = jnp.dot(tiles, spread, preferred_element_type=jnp.float32).astype(jnp.bfloat16)
        live = jnp.dot(by_row, tiles, preferred_element_type=jnp.float32)
        live = jnp.where(own_lane, live, 0.0).astype(jnp.bfloat16)
        live = jnp.dot(live, ones, preferred_element_type=jnp.float32)
        ok = near_cols & (jnp.abs(k_row + b * rows - q_row) <= R) & (live > 0.5) & inside
        if blocks[i] == 0:
            ok = ok | ((k_row == q_row) & (k_col == q_col))
        bias_ref[at_b, :] = jnp.where(ok, 0.0, NEG)
        if copies:
            copies[i].wait()
        for g in range(GROUPS):
            w0 = WIN_START[g]
            k_win = ref[0, :, :, w0 : w0 + WIN].reshape(keys, WIN)
            s_ref[at_b, g * stacked : (g + 1) * stacked] = lax.dot_general(
                k_win, stacks[g], NT, preferred_element_type=jnp.float32
            )
        put_transposed(vt_ref, i * keys, ref[1].reshape(keys, width))
    for h in range(HEAD_COUNT):
        s = s_ref[:, h * queries : (h + 1) * queries] * (LOG2E / math.sqrt(dh)) + bias_ref[...]
        top = jnp.maximum(jnp.max(s, axis=0, keepdims=True), 0.1 * NEG)
        p = jnp.exp2(s - top)
        top_ref[h : h + 1, :] = top
        total_ref[h : h + 1, :] = jnp.sum(p, axis=0, keepdims=True)
        out_ref[h * dh : (h + 1) * dh, :] = jnp.dot(
            vt_ref[h * dh : (h + 1) * dh, :], p.astype(jnp.bfloat16), preferred_element_type=jnp.float32
        )


def merge_kernel(
    own_ref, own_top_ref, own_total_ref, far_ref, far_top_ref, far_total_ref, back_ref, weight_ref, out_ref,
    bt_ref, at_ref,
):
    rows, cols, width = out_ref.shape
    queries = rows * cols
    dh = width // HEAD_COUNT
    put_transposed(bt_ref, 0, back_ref[...].reshape(queries, width + 128))
    lse = bt_ref[width : width + HEAD_COUNT, :]
    for part in range(1, STATS):
        lse = lse + bt_ref[width + part * HEAD_COUNT : width + (part + 1) * HEAD_COUNT, :]
    big = jnp.maximum(jnp.maximum(own_top_ref[...], far_top_ref[...]), lse)
    a = jnp.exp2(own_top_ref[...] - big)
    b = jnp.exp2(far_top_ref[...] - big)
    c = jnp.exp2(lse - big)
    inverse = 1.0 / (a * own_total_ref[...] + b * far_total_ref[...] + c)
    a, b, c = a * inverse, b * inverse, c * inverse
    for h in range(HEAD_COUNT):
        at = slice(h * dh, (h + 1) * dh)
        one = slice(h, h + 1)
        at_ref[at, :] = a[one] * own_ref[at, :] + b[one] * far_ref[at, :] + c[one] * bt_ref[at, :]
    att = jnp.concatenate(
        [at_ref[t * 128 : (t + 1) * 128, :].T.astype(jnp.bfloat16) for t in range(width // 128)], axis=1
    )
    enc = jnp.dot(att, weight_ref[...], preferred_element_type=jnp.float32)
    out_ref[...] = enc.astype(jnp.bfloat16).reshape(out_ref.shape)


def call(kernel, out_shape, ins, scratch=(), flops=0, outs=None):
    spaces = dict(v=pltpu.VMEM, h=pltpu.HBM)
    many = isinstance(out_shape, (tuple, list))
    return pl.pallas_call(
        kernel,
        out_shape=out_shape,
        in_specs=[pl.BlockSpec(memory_space=spaces[c]) for c in ins],
        out_specs=[pl.BlockSpec(memory_space=spaces[c]) for c in outs or "v" * len(out_shape)]
        if many
        else pl.BlockSpec(memory_space=pltpu.VMEM),
        scratch_shapes=list(scratch),
        cost_estimate=pl.CostEstimate(flops=flops, transcendentals=0, bytes_accessed=1 << 20),
        compiler_params=pltpu.CompilerParams(vmem_limit_bytes=24 << 20),
    )


def partners(count, first):
    low = range(first, count - 1, 2)
    return [(i, i + 1) for i in low] + [(i + 1, i) for i in low]


def per_device(q, k, v, tissue, dilation_levels, segment_levels, weight):
    rows, cols, width = q.shape
    peers = lax.axis_size("col")
    n_row = lax.axis_size("row")
    bf16, f32 = jnp.bfloat16, jnp.float32
    shape, vmem = jax.ShapeDtypeStruct, pltpu.VMEM
    slots = peers * KEYS
    x_groups = [[z * X + x for x in range(X)] for z in range(peers // X)]
    half = shape((2, rows, R, width), bf16)
    hbm = [pltpu.with_memory_space_constraint(x, pltpu.HBM) for x in (dilation_levels, segment_levels, k, v, tissue)]
    hbm.append(pltpu.with_memory_space_constraint(q.reshape(X, 2 * cols, width), pltpu.HBM))
    send, first, second, ok = call(
        pack_kernel,
        [shape((X, 2 * cols + SLOTS, width), bf16), half, half, shape((128, slots), f32)],
        ins="hhhhhh",
        outs="hvvv",
        scratch=[vmem((rows, cols, width), bf16)] * 2
        + [vmem((rows, tissue.shape[1]), jnp.int32)]
        + [pltpu.SMEM((HEAD_COUNT,), jnp.int32)] * 2
        + [vmem((X, 2 * cols, width), bf16), vmem((X, SLOTS, width), bf16), pltpu.SemaphoreType.DMA((8,))],
    )(*hbm)
    stripe = lax.all_to_all(send, "col", 0, 0, tiled=True, axis_index_groups=x_groups)
    z_groups = [[z * X + x for z in range(peers // X)] for x in range(X)]
    got = jnp.broadcast_to(stripe[None, :, 2 * cols :], (peers // X, X, SLOTS, width))
    got = lax.all_to_all(got.reshape(peers, SLOTS, width), "col", 0, 0, tiled=True, axis_index_groups=z_groups)
    from_first = lax.ppermute(first, "col", partners(peers, 0))
    from_second = lax.ppermute(second, "col", partners(peers, 1))
    own = jnp.concatenate([from_second, jnp.stack([k, v]), from_first], axis=2)
    above = lax.ppermute(own, "row", partners(n_row, 0))
    below = lax.ppermute(own, "row", partners(n_row, 1))
    queries = rows * cols
    stack = HEAD_COUNT * queries
    back = call(
        dilated_kernel,
        shape((rows, cols, width + 128), bf16),
        ins="vvv",
        scratch=[
            vmem((slots, stack), f32),
            vmem((slots, width), f32),
            vmem((width, slots), bf16),
            vmem((width + 128, queries), f32),
        ],
        flops=1 << 31,
    )(stripe, got, ok)
    back = lax.all_to_all(back, "col", 0, 0, tiled=True, axis_index_groups=x_groups)
    keys = rows * (cols + 2 * R)
    per_head = shape((HEAD_COUNT, queries), f32)

    def window(blocks, sources, ins, extra=()):
        n = len(blocks) * keys
        return call(
            functools.partial(window_kernel, blocks=blocks),
            [shape((width, queries), f32), per_head, per_head],
            ins="vv" + ins,
            scratch=[vmem((n, queries), f32), vmem((n, stack), f32), vmem((width, n), bf16), *extra],
            flops=len(blocks) << 31,
        )(q, tissue, *sources)

    own_parts = window((0,), (own,), "v")
    above, below = (pltpu.with_memory_space_constraint(x, pltpu.HBM) for x in (above, below))
    extra = [vmem(own.shape, bf16)] * 2 + [pltpu.SemaphoreType.DMA((2,))]
    far_parts = window((1, -1), (above, below), "hh", extra)
    return call(
        merge_kernel,
        shape((rows, cols, width), bf16),
        ins="v" * 8,
        scratch=[vmem((width + 128, queries), f32), vmem((width, queries), f32)],
        flops=1 << 28,
    )(*own_parts, *far_parts, back, weight)


def solution(mesh):
    spec = P("row", "col", None)
    return jax.shard_map(
        per_device,
        mesh=mesh,
        in_specs=(spec, spec, spec, P(), P(), P(), P()),
        out_specs=spec,
        check_vma=False,
    )
```
